32 devices in a mesh: sp: 8 (over y, x, core), ch: 4 (over z).
Axes of the slice: x: 2, y: 2, z: 4, core: 2. Of those that a mesh axis runs over, the one named last changes fastest.
Arguments:
- features: bfloat16 [64, 64, 2, 2, 14, 128], P(None, ('sp', 'ch')), may hold values from -6 to 6
- pre_act: bfloat16 [128, 32, 14, 128], P(None, ('sp', 'ch')), may hold values from -6 to 6
- cotangent: bfloat16 [128, 32, 14, 128], P(None, ('sp', 'ch')), may hold values from -12 to 12
- weight: bfloat16 [27, 64, 128], replicated, may hold values from -0.15625 to 0.15625
Outputs:
- data_grad: bfloat16 [64, 64, 2, 2, 14, 128], P(None, ('sp', 'ch'))
- weight_grad: float32 [27, 64, 128], replicated
The draws below stay inside these ranges and needn't reach their ends.
All inputs are finite; a program needn't handle non-finite values.
Results may differ from the reference program's by a relative error of at most 0.0025.
Values may be sent and summed in bfloat16 or wider, within the bound.
A program may use at most 64 MiB of HBM per device.

```python
import math
import jax
import jax.numpy as jnp
from jax import lax

C_IN = 64
C_OUT = 128
TAPS = 27
ROWS_OUT = 14
COLS_OUT = 128
DEP_OUT = 32
DEPTH = 64
OUT_VOX = 57344


def levels(rng, dims, split, smallest, top_value):
    factor_of = 1.0
    for position, shards_of in split:
        heights = jax.random.uniform(jax.random.fold_in(jax.random.fold_in(rng, 6), position), (shards_of,), jnp.float32, smallest / len(split), top_value / len(split))
        factor_of = factor_of * jnp.repeat(jnp.exp(heights), dims[position] // shards_of).reshape((-1,) + (1,) * (len(dims) - 1 - position))
    return factor_of


def centred(own_key, extent, scale, limit, split=(), kind=jnp.bfloat16):
    gain = levels(own_key, extent, split, -0.22, 0.18) if split else 1.0
    values = jax.random.normal(own_key, extent, jnp.float32) * scale * gain
    return jnp.minimum(jnp.maximum(values, -limit), limit).astype(kind)


def setup_inputs(seed: int = 0) -> dict:
    seeds = jax.random.split(jax.random.key(seed), 5)
    return {
        "features": centred(seeds[0], (C_IN, DEPTH, 2, 2, ROWS_OUT, COLS_OUT), 1.0, 6.0, ((1, 32),)),
        "pre_act": centred(seeds[1], (C_OUT, DEP_OUT, ROWS_OUT, COLS_OUT), 1.0, 6.0, ((1, 32),)),
        "cotangent": centred(seeds[2], (C_OUT, DEP_OUT, ROWS_OUT, COLS_OUT), 2.0, 12.0, ((1, 32),)),
        "weight": centred(seeds[3], (TAPS, C_IN, C_OUT), (TAPS * C_IN) ** -0.5, 0.15625),
    }


def shifted(grad_plane, down, right):
    if down:
        grad_plane = jnp.concatenate([grad_plane[:, 1:], jnp.zeros_like(grad_plane[:, :1])], 1)
    if right:
        grad_plane = jnp.concatenate([grad_plane[..., 1:], jnp.zeros_like(grad_plane[..., :1])], -1)
    return grad_plane

def shift_set(grad_plane):
    result = {}
    for down in (0, 1):
        for right in (0, 1):
            result[down, right] = shifted(grad_plane, down, right).reshape(grad_plane.shape[0], -1)
    return result

def tap_parts(tap_pos):
    return (0 if tap_pos == 1 else 1, 1 if tap_pos == 0 else 0)

def weight_terms(depth_planes, grad_set, depth_taps):
    tap_terms = []
    for depth_tap in depth_taps:
        plane = depth_planes[depth_tap]
        for row_tap in range(3):
            row_par, down = tap_parts(row_tap)
            for col_tap in range(3):
                col_par, right = tap_parts(col_tap)
                tap_rows = plane[:, row_par, col_par].reshape(plane.shape[0], -1)
                tap_terms.append(lax.dot_general(tap_rows, grad_set[down, right], (((1,), (1,)), ((), ())), preferred_element_type=jnp.float32))
    return jnp.stack(tap_terms)

def data_terms(weight, here_set, next_set, out_rows, out_cols):
    chans = weight.shape[1]
    groups = {}
    for depth_tap in range(3):
        depth_par = 0 if depth_tap == 1 else 1
        source = next_set if depth_tap == 0 else here_set
        for row_tap in range(3):
            row_par, down = tap_parts(row_tap)
            for col_tap in range(3):
                col_par, right = tap_parts(col_tap)
                key = (depth_par, row_par, col_par)
                if key not in groups:
                    groups[key] = ([], [])
                groups[key][0].append(weight[depth_tap * 9 + row_tap * 3 + col_tap])
                groups[key][1].append(source[down, right])
    results = {}
    for key, pair in groups.items():
        w_rows = jnp.concatenate(pair[0], 1)
        results[key] = jnp.dot(w_rows, jnp.concatenate(pair[1], 0), preferred_element_type=jnp.float32).reshape(chans, out_rows, out_cols)
    depth_parts = []
    for depth_par in range(2):
        row_parts = []
        for row_par in range(2):
            row_parts.append(jnp.stack([results[depth_par, row_par, 0], results[depth_par, row_par, 1]], 1))
        depth_parts.append(jnp.stack(row_parts, 1))
    return jnp.stack(depth_parts, 1).astype(jnp.bfloat16)

def reference(features, pre_act, cotangent, weight):
    masked = jnp.where(pre_act > 0, cotangent, jnp.zeros_like(cotangent))
    padded_in = jnp.pad(features, ((0, 0), (1, 0), (0, 0), (0, 0), (0, 0), (0, 0)))
    padded_out = jnp.pad(masked, ((0, 0), (0, 1), (0, 0), (0, 0)))

    def step(total, block_id):
        start_in = (block_id * 2).astype(jnp.int32)
        prev_plane = lax.dynamic_slice_in_dim(padded_in, start_in, 1, 1)[:, 0]
        block = lax.dynamic_slice_in_dim(features, start_in, 2, 1)
        here = lax.dynamic_slice_in_dim(masked, block_id.astype(jnp.int32), 1, 1)[:, 0]
        after = lax.dynamic_slice_in_dim(padded_out, (block_id + 1).astype(jnp.int32), 1, 1)[:, 0]
        here_set = shift_set(here)
        next_set = shift_set(after)
        planes = {0: prev_plane, 1: block[:, 0], 2: block[:, 1]}
        total = total + weight_terms(planes, here_set, (0, 1, 2))
        return (total, data_terms(weight, here_set, next_set, ROWS_OUT, COLS_OUT))
    start = jnp.zeros((TAPS, C_IN, C_OUT), jnp.float32)
    raw, pieces = lax.scan(step, start, jnp.arange(DEP_OUT, dtype=jnp.int32))
    data_grad = jnp.moveaxis(pieces, 0, 1).reshape(C_IN, DEPTH, 2, 2, ROWS_OUT, COLS_OUT)
    weight_grad = raw * (1.0 / math.sqrt(OUT_VOX))
    return (data_grad, weight_grad)
```

```python
import functools
import math

import jax
import jax.numpy as jnp
from jax import lax
from jax.experimental import pallas as pl
from jax.experimental.pallas import tpu as pltpu
from jax.sharding import PartitionSpec as P

MESH = pl.DeviceIdType.MESH
LANES = 128
UNIT = 8


def kernel(cfg, pre_hbm, cot_hbm, feat_hbm, w_hbm, dg_out, wg_out, *scr):
    (pre_v, cot_v, feat_v, w_v, m_nat, h_nat, mh, mn, feat_a, wl, wf, ws, dg_v, grad, own_a, own_b) = scr[:16]
    (r1a, r1b, r2a, r2b, r3a, r3b) = scr[16:22]
    in_sem, out_sem, halo_s, halo_r, send_sem, recv_sem = scr[22:]
    chips, chs, rows, c_in, c_out, scale, groups = cfg
    sp = lax.axis_index("sp")
    ch = lax.axis_index("ch")
    chip = sp // 2
    core = sp % 2
    flat = sp * chs + ch
    last = chips * 2 * chs - 1
    span = rows * LANES

    def chip_dev(k, c):
        return (((chip + k) % chips) * 2 + c, ch)

    def ch_dev(k):
        return (sp, (ch + k) % chs)

    bar = pltpu.get_barrier_semaphore()
    prev = jnp.maximum(flat - 1, 0)
    nxt = jnp.minimum(flat + 1, last)

    @pl.when(flat > 0)
    def _():
        pl.semaphore_signal(bar, inc=1, device_id=(prev // chs, prev % chs), device_id_type=MESH)

    @pl.when(flat < last)
    def _():
        pl.semaphore_signal(bar, inc=1, device_id=(nxt // chs, nxt % chs), device_id_type=MESH)

    loads = [
        pltpu.make_async_copy(pre_hbm.at[0], pre_v, in_sem.at[0]),
        pltpu.make_async_copy(cot_hbm.at[0], cot_v, in_sem.at[1]),
        pltpu.make_async_copy(w_hbm, w_v, in_sem.at[2]),
    ]
    loads[0].start()
    loads[1].start()
    for k in range(1, chs):
        pl.semaphore_signal(bar, inc=1, device_id=ch_dev(k), device_id_type=MESH)
    for k in range(1, chips):
        pl.semaphore_signal(bar, inc=1, device_id=chip_dev(k, core), device_id_type=MESH)
    for k in range(chips):
        pl.semaphore_signal(bar, inc=1, device_id=chip_dev(k, 1 - core), device_id_type=MESH)
    loads[2].start()

    def load_feat(k, carry):
        p, s, b = k // (2 * rows), (k // rows) % 2, k % rows
        pltpu.make_async_copy(feat_hbm.at[:, p, s, b], feat_v.at[p, s, b], in_sem.at[3]).start()
        return carry

    lax.fori_loop(0, 4 * rows, load_feat, 0)

    loads[0].wait()
    loads[1].wait()

    def mask_step(b, carry):
        p = pre_v[b].astype(jnp.float32)
        m_nat[b] = jnp.where(p > 0, cot_v[b].astype(jnp.float32), 0.0).astype(jnp.bfloat16)
        return carry

    lax.fori_loop(0, rows, mask_step, 0)
    peers = 2 * chips + chs - 2 + jnp.minimum(flat, 1) + jnp.minimum(last - flat, 1)
    pl.semaphore_wait(bar, peers)

    halo = pltpu.make_async_remote_copy(
        src_ref=m_nat, dst_ref=h_nat, send_sem=halo_s, recv_sem=halo_r,
        device_id=(prev // chs, prev % chs), device_id_type=MESH,
    )

    @pl.when(flat > 0)
    def _():
        halo.start()

    lane = lax.broadcasted_iota(jnp.int32, (c_out, LANES), 1)

    def spread(src, dst):
        dst[:, span:] = jnp.zeros((2 * c_out, LANES), jnp.bfloat16)
        for b in range(rows):
            v = src[b]
            dst[:c_out, b * LANES:(b + 1) * LANES] = v
            r = jnp.where(lane == LANES - 1, 0.0, pltpu.roll(v.astype(jnp.float32), LANES - 1, 1))
            dst[c_out:, b * LANES:(b + 1) * LANES] = r.astype(jnp.bfloat16)

    spread(m_nat, mh)
    pltpu.make_async_copy(feat_v, feat_v, in_sem.at[3]).wait()
    two = 2 * c_in

    feat_rows = feat_v.reshape(2, 2, rows, two, LANES)

    def feat_step(k, carry):
        p, s = k // 2, k % 2
        at = pl.ds(pl.multiple_of(s * two, two), two)
        for b in range(rows):
            feat_a[p, at, b * LANES:(b + 1) * LANES] = feat_rows[p, s, b]
        return carry

    lax.fori_loop(0, 4, feat_step, 0)

    ups = c_in // UNIT
    starts = {0: groups[1][0], 1: groups[0][0], 2: groups[0][0] + 9 * ups}

    def put(kd, kh, kw, val):
        base = starts[kd] + (kh * 3 + kw) * ups
        grad[base:base + ups] = val.reshape(ups, UNIT, c_out)

    def wgrad(kd, p, mm):
        dn = (((1,), (1,)), ((), ()))
        o = lax.dot_general(feat_a[p], mm[:, :span], dn, preferred_element_type=jnp.float32)
        d = lax.dot_general(feat_a[p, two:], mm[:, LANES:], dn, preferred_element_type=jnp.float32)
        for r in range(2):
            ws[r, :2 * two] = o[:, r * c_out:(r + 1) * c_out]
            ws[r, 2 * two:] = d[:, r * c_out:(r + 1) * c_out]
        for kh, part in ((1, 0), (2, 1), (0, 2)):
            for kw, r, t in ((1, 0, 0), (2, 0, 1), (0, 1, 1)):
                put(kd, kh, kw, ws[r, pl.ds(part * two + t, c_in, stride=2), :])

    def weights():
        def step(kd, carry):
            for part, kh in enumerate((1, 2, 0)):
                base = kd * 9 + kh * 3
                wf[0, pl.ds(0, c_in, stride=2), :] = w_v[base + 1].astype(jnp.float32)
                wf[0, pl.ds(1, c_in, stride=2), :] = w_v[base + 2].astype(jnp.float32)
                wf[1, pl.ds(0, c_in, stride=2), :] = jnp.zeros((c_in, c_out), jnp.float32)
                wf[1, pl.ds(1, c_in, stride=2), :] = w_v[base].astype(jnp.float32)
                for r in range(2):
                    wl[kd, part * two:(part + 1) * two, r * c_out:(r + 1) * c_out] = wf[r].astype(jnp.bfloat16)
            return carry

        lax.fori_loop(0, 3, step, 0)

    dg_rows = dg_v.reshape(2, 2, rows, two, LANES)

    def dgrad(p, terms, lo, hi):
        def step(k, carry):
            col = pl.multiple_of(k * 2 * LANES, 2 * LANES)
            here = pl.ds(col, 2 * LANES)
            down = pl.ds(pl.multiple_of(col + LANES, LANES), 2 * LANES)
            top, bot = None, None
            for kd, mm in terms:
                o = jnp.dot(wl[kd, :2 * two], mm[:, here], preferred_element_type=jnp.float32)
                d = jnp.dot(wl[kd, 2 * two:], mm[:, down], preferred_element_type=jnp.float32)
                top = o[:two] if top is None else top + o[:two]
                bot = o[two:] + d if bot is None else bot + (o[two:] + d)
            for s, val in ((0, top), (1, bot)):
                for j in range(2):
                    b = 2 * k + j
                    dg_rows[p, s, b] = val[:, j * LANES:(j + 1) * LANES].astype(jnp.bfloat16)
                    pltpu.make_async_copy(dg_v.at[p, s, b], dg_out.at[:, p, s, b], out_sem.at[0]).start()
            return carry

        lax.fori_loop(lo, hi, step, 0)

    class Reduce:
        def __init__(self, idx, r1, r2, r3, own):
            self.i, self.r1, self.r2, self.r3, self.own = idx, r1, r2, r3, own
            self.base, self.u = groups[idx]
            self.half = self.u * chips
            self.copies = {}

        def off(self, a, b):
            return self.base + a * self.half + b * self.u

        def remote(self, stage, src, dst, dev):
            return pltpu.make_async_remote_copy(
                src_ref=src, dst_ref=dst, send_sem=send_sem.at[self.i, stage - 1],
                recv_sem=recv_sem.at[self.i, stage - 1], device_id=dev, device_id_type=MESH)

        def start(self, stage):
            cps = []
            if stage == 1:
                src = grad.at[pl.ds(self.off(1 - core, 0), self.half)]
                cps.append(self.remote(1, src, self.r1, chip_dev(0, 1 - core)))
            elif stage == 2:
                for k in range(1, chips):
                    src = grad.at[pl.ds(self.off(core, (chip + k) % chips), self.u)]
                    cps.append(self.remote(2, src, self.r2.at[k - 1], chip_dev(k, core)))
            elif stage == 3:
                for k in range(1, chs):
                    cps.append(self.remote(3, self.r3.at[ch], self.r3.at[ch], ch_dev(k)))
            else:
                dst = wg_out.at[pl.ds(self.off(core, chip), self.u)]
                for k in range(1, chips):
                    cps.append(self.remote(4, self.own, dst, chip_dev(k, core)))
                for k in range(chips):
                    cps.append(self.remote(4, self.own, dst, chip_dev(k, 1 - core)))
                self.local = pltpu.make_async_copy(self.own, dst, out_sem.at[1 + self.i])
                self.local.start()
            for c in cps:
                c.start()
            self.copies[stage] = cps

        def finish(self, stage):
            if stage == 1:
                self.copies[1][0].wait()
                s = pl.ds(self.off(core, 0), self.half)
                grad[s] = grad[s] + self.r1[...]
            elif stage == 2:
                whole = pltpu.make_async_remote_copy(
                    src_ref=self.r2, dst_ref=self.r2, send_sem=send_sem.at[self.i, 1],
                    recv_sem=recv_sem.at[self.i, 1], device_id=(sp, ch), device_id_type=MESH)
                whole.wait_send()
                whole.wait_recv()
                v = grad[pl.ds(self.off(core, chip), self.u)]
                for k in range(chips - 1):
                    v = v + self.r2[k]
                self.r3[ch] = v
            elif stage == 3:
                most = self.r3.at[pl.ds(0, chs - 1)]
                whole = pltpu.make_async_remote_copy(
                    src_ref=most, dst_ref=most, send_sem=send_sem.at[self.i, 2],
                    recv_sem=recv_sem.at[self.i, 2], device_id=(sp, ch), device_id_type=MESH)
                whole.wait_send()
                whole.wait_recv()
                v = self.r3[0]
                for k in range(1, chs):
                    v = v + self.r3[k]
                self.own[...] = v * scale
            else:
                most = wg_out.at[pl.ds(self.base, (2 * chips - 1) * self.u)]
                whole = pltpu.make_async_remote_copy(
                    src_ref=most, dst_ref=most, send_sem=send_sem.at[self.i, 3],
                    recv_sem=recv_sem.at[self.i, 3], device_id=(sp, ch), device_id_type=MESH)
                whole.wait_send()
                whole.wait_recv()
                self.local.wait()

    red_a = Reduce(0, r1a, r2a, r3a, own_a)
    red_b = Reduce(1, r1b, r2b, r3b, own_b)

    for idx, taps in ((0, 18), (1, 9)):
        lo, hi = groups[idx][0] + taps * ups, groups[idx][0] + groups[idx][1] * 2 * chips
        if lo < hi:
            grad[lo:hi] = jnp.zeros((hi - lo, UNIT, LANES), jnp.float32)

    def halo_done():
        @pl.when(flat > 0)
        def _():
            halo.wait_send()

        @pl.when(flat < last)
        def _():
            halo.wait_recv()

        @pl.when(flat == last)
        def _():
            h_nat[...] = jnp.zeros_like(h_nat)

    half = rows // 2
    both = [(2, mh), (0, mn)]

    wgrad(1, 0, mh)
    wgrad(2, 1, mh)
    red_a.start(1)
    loads[2].wait()
    weights()
    red_a.finish(1)
    red_a.start(2)
    dgrad(0, [(1, mh)], 0, half)
    halo_done()
    spread(h_nat, mn)
    wgrad(0, 1, mn)
    red_b.start(1)
    red_a.finish(2)
    red_a.start(3)
    red_b.finish(1)
    red_b.start(2)
    dgrad(1, both, 0, half)
    red_b.finish(2)
    red_b.start(3)
    red_a.finish(3)
    red_a.start(4)
    red_b.finish(3)
    red_b.start(4)
    red_a.finish(4)
    red_b.finish(4)
    pltpu.make_async_copy(dg_v, dg_v, out_sem.at[0]).wait()


def store_kernel(groups, ups, dg_in, wg_in, dg_out, wg_out, sem):
    copies = [
        pltpu.make_async_copy(dg_in, dg_out, sem.at[0]),
        pltpu.make_async_copy(wg_in.at[pl.ds(groups[1][0], 9 * ups)], wg_out.at[pl.ds(0, 9 * ups)], sem.at[1]),
        pltpu.make_async_copy(wg_in.at[pl.ds(groups[0][0], 18 * ups)], wg_out.at[pl.ds(9 * ups, 18 * ups)], sem.at[2]),
    ]
    for c in copies:
        c.start()
    for c in copies:
        c.wait()


def on_device(features, pre_act, cotangent, weight):
    c_in, planes_in, _, _, rows, cols = features.shape
    c_out, planes = pre_act.shape[:2]
    taps = weight.shape[0]
    chips = lax.axis_size("sp") // 2
    chs = lax.axis_size("ch")
    devices = chips * 2 * chs
    scale = 1.0 / math.sqrt(devices * planes * rows * cols)
    ups = c_in // UNIT
    u_a = -(-18 * ups // (2 * chips))
    u_b = -(-9 * ups // (2 * chips))
    groups = ((u_b * 2 * chips, u_a), (0, u_b))
    units = (u_a + u_b) * 2 * chips
    cfg = (chips, chs, rows, c_in, c_out, scale, groups)
    bf, f32 = jnp.bfloat16, jnp.float32
    span = rows * cols
    any_spec = pl.BlockSpec(memory_space=pl.ANY)

    def part(*lead):
        return pltpu.VMEM(lead + (UNIT, c_out), f32)

    held = 2 * units + (u_a + u_b) * (2 * chips + chs)
    vmem = 17 * 2**20 + held * UNIT * c_out * 4
    dg, wg = pl.pallas_call(
        functools.partial(kernel, cfg),
        out_shape=(
            jax.ShapeDtypeStruct((c_in, 2, 2, rows, 2, cols), bf),
            jax.ShapeDtypeStruct((units, UNIT, c_out), f32),
        ),
        in_specs=[pl.BlockSpec(memory_space=pltpu.HBM)] * 4,
        out_specs=(any_spec, any_spec),
        scratch_shapes=[
            pltpu.VMEM((rows, c_out, cols), bf),
            pltpu.VMEM((rows, c_out, cols), bf),
            pltpu.VMEM((2, 2, rows, c_in, 2, cols), bf),
            pltpu.VMEM(weight.shape, bf),
            pltpu.VMEM((rows, c_out, cols), bf),
            pltpu.VMEM((rows, c_out, cols), bf),
            pltpu.VMEM((2 * c_out, span + cols), bf),
            pltpu.VMEM((2 * c_out, span + cols), bf),
            pltpu.VMEM((2, 4 * c_in, span), bf),
            pltpu.VMEM((3, 6 * c_in, 2 * c_out), bf),
            pltpu.VMEM((2, 2 * c_in, c_out), f32),
            pltpu.VMEM((2, 6 * c_in, c_out), f32),
            pltpu.VMEM((2, 2, rows, c_in, 2, cols), bf),
            part(units),
            part(u_a),
            part(u_b),
            part(u_a * chips),
            part(u_b * chips),
            part(chips - 1, u_a),
            part(chips - 1, u_b),
            part(chs, u_a),
            part(chs, u_b),
            pltpu.SemaphoreType.DMA((4,)),
            pltpu.SemaphoreType.DMA((3,)),
            pltpu.SemaphoreType.DMA,
            pltpu.SemaphoreType.DMA,
            pltpu.SemaphoreType.DMA((2, 4)),
            pltpu.SemaphoreType.DMA((2, 4)),
        ],
        compiler_params=pltpu.CompilerParams(
            collective_id=0, has_side_effects=True, vmem_limit_bytes=vmem
        ),
    )(
        pltpu.with_memory_space_constraint(pre_act.transpose(1, 2, 0, 3), pltpu.HBM),
        pltpu.with_memory_space_constraint(cotangent.transpose(1, 2, 0, 3), pltpu.HBM),
        pltpu.with_memory_space_constraint(features.transpose(0, 1, 2, 4, 3, 5), pltpu.HBM),
        pltpu.with_memory_space_constraint(weight, pltpu.HBM),
    )
    dg, wg = pl.pallas_call(
        functools.partial(store_kernel, groups, ups),
        out_shape=(
            jax.ShapeDtypeStruct((c_in, planes_in, 2, rows, 2, cols), bf),
            jax.ShapeDtypeStruct((taps * ups, UNIT, c_out), f32),
        ),
        in_specs=[any_spec] * 2,
        out_specs=(pl.BlockSpec(memory_space=pltpu.HBM),) * 2,
        scratch_shapes=[pltpu.SemaphoreType.DMA((3,))],
        compiler_params=pltpu.CompilerParams(vmem_limit_bytes=2**20),
    )(dg, wg)
    return dg.transpose(0, 1, 2, 4, 3, 5), wg.reshape(taps, c_in, c_out)


def solution(mesh):
    return jax.shard_map(
        on_device,
        mesh=mesh,
        in_specs=(
            P(None, ("sp", "ch"), None, None, None, None),
            P(None, ("sp", "ch"), None, None),
            P(None, ("sp", "ch"), None, None),
            P(),
        ),
        out_specs=(P(None, ("sp", "ch"), None, None, None, None), P()),
        check_vma=False,
    )
```

```python
import functools
import math

import jax
import jax.numpy as jnp
from jax import lax
from jax.experimental import pallas as pl
from jax.experimental.pallas import tpu as pltpu
from jax.sharding import PartitionSpec as P

MESH = pl.DeviceIdType.MESH
LANES = 128
UNIT = 8


def kernel(cfg, pre_hbm, cot_hbm, feat_hbm, w_hbm, dg_out, wg_out, *scr):
    (pre_v, cot_v, feat_v, w_v, m_nat, h_nat, mh, mn, feat_a, wl, wf, ws, dg_v, grad, own_a, own_b) = scr[:16]
    (r1a, r1b, r2a, r2b, mid_a, r3a, r3b) = scr[16:23]
    in_sem, out_sem, halo_s, halo_r, send_sem, recv_sem = scr[23:]
    chips, chs, rows, c_in, c_out, scale, groups = cfg
    sp = lax.axis_index("sp")
    ch = lax.axis_index("ch")
    chip = sp // 2
    core = sp % 2
    flat = sp * chs + ch
    last = chips * 2 * chs - 1
    span = rows * LANES

    def chip_dev(k, c):
        return (((chip + k) % chips) * 2 + c, ch)

    def ch_dev(k):
        return (sp, (ch + k) % chs)

    bar = pltpu.get_barrier_semaphore()
    prev = jnp.maximum(flat - 1, 0)
    nxt = jnp.minimum(flat + 1, last)

    @pl.when(flat > 0)
    def _():
        pl.semaphore_signal(bar, inc=1, device_id=(prev // chs, prev % chs), device_id_type=MESH)

    @pl.when(flat < last)
    def _():
        pl.semaphore_signal(bar, inc=1, device_id=(nxt // chs, nxt % chs), device_id_type=MESH)

    loads = [
        pltpu.make_async_copy(pre_hbm.at[0], pre_v, in_sem.at[0]),
        pltpu.make_async_copy(cot_hbm.at[0], cot_v, in_sem.at[1]),
        pltpu.make_async_copy(w_hbm, w_v, in_sem.at[2]),
    ]
    loads[0].start()
    loads[1].start()
    for k in range(1, chs):
        pl.semaphore_signal(bar, inc=1, device_id=ch_dev(k), device_id_type=MESH)
    for k in range(1, chips):
        pl.semaphore_signal(bar, inc=1, device_id=chip_dev(k, core), device_id_type=MESH)
    for k in range(chips):
        pl.semaphore_signal(bar, inc=1, device_id=chip_dev(k, 1 - core), device_id_type=MESH)
    loads[2].start()

    def load_feat(k, carry):
        p, s, b = k // (2 * rows), (k // rows) % 2, k % rows
        pltpu.make_async_copy(feat_hbm.at[:, p, s, b], feat_v.at[p, s, b], in_sem.at[3]).start()
        return carry

    lax.fori_loop(0, 4 * rows, load_feat, 0)

    loads[0].wait()
    loads[1].wait()

    def mask_step(b, carry):
        p = pre_v[b].astype(jnp.float32)
        m_nat[b] = jnp.where(p > 0, cot_v[b].astype(jnp.float32), 0.0).astype(jnp.bfloat16)
        return carry

    lax.fori_loop(0, rows, mask_step, 0)
    peers = 2 * chips + chs - 2 + jnp.minimum(flat, 1) + jnp.minimum(last - flat, 1)
    pl.semaphore_wait(bar, peers)

    halo = pltpu.make_async_remote_copy(
        src_ref=m_nat, dst_ref=h_nat, send_sem=halo_s, recv_sem=halo_r,
        device_id=(prev // chs, prev % chs), device_id_type=MESH,
    )

    @pl.when(flat > 0)
    def _():
        halo.start()

    lane = lax.broadcasted_iota(jnp.int32, (c_out, LANES), 1)

    def spread(src, dst):
        dst[:, span:] = jnp.zeros((2 * c_out, LANES), jnp.bfloat16)
        for b in range(rows):
            v = src[b]
            dst[:c_out, b * LANES:(b + 1) * LANES] = v
            r = jnp.where(lane == LANES - 1, 0.0, pltpu.roll(v.astype(jnp.float32), LANES - 1, 1))
            dst[c_out:, b * LANES:(b + 1) * LANES] = r.astype(jnp.bfloat16)

    spread(m_nat, mh)
    pltpu.make_async_copy(feat_v, feat_v, in_sem.at[3]).wait()
    two = 2 * c_in

    feat_rows = feat_v.reshape(2, 2, rows, two, LANES)

    def feat_step(k, carry):
        p, s = k // 2, k % 2
        at = pl.ds(pl.multiple_of(s * two, two), two)
        for b in range(rows):
            feat_a[p, at, b * LANES:(b + 1) * LANES] = feat_rows[p, s, b]
        return carry

    lax.fori_loop(0, 4, feat_step, 0)

    ups = c_in // UNIT
    starts = {0: groups[1][0], 1: groups[0][0], 2: groups[0][0] + 9 * ups}

    def put(kd, kh, kw, val):
        base = starts[kd] + (kh * 3 + kw) * ups
        grad[base:base + ups] = val.reshape(ups, UNIT, c_out)

    def wgrad(kd, p, mm):
        dn = (((1,), (1,)), ((), ()))
        o = lax.dot_general(feat_a[p], mm[:, :span], dn, preferred_element_type=jnp.float32)
        d = lax.dot_general(feat_a[p, two:], mm[:, LANES:], dn, preferred_element_type=jnp.float32)
        for r in range(2):
            ws[r, :2 * two] = o[:, r * c_out:(r + 1) * c_out]
            ws[r, 2 * two:] = d[:, r * c_out:(r + 1) * c_out]
        for kh, part in ((1, 0), (2, 1), (0, 2)):
            for kw, r, t in ((1, 0, 0), (2, 0, 1), (0, 1, 1)):
                put(kd, kh, kw, ws[r, pl.ds(part * two + t, c_in, stride=2), :])

    def weights():
        def step(kd, carry):
            for part, kh in enumerate((1, 2, 0)):
                base = kd * 9 + kh * 3
                wf[0, pl.ds(0, c_in, stride=2), :] = w_v[base + 1].astype(jnp.float32)
                wf[0, pl.ds(1, c_in, stride=2), :] = w_v[base + 2].astype(jnp.float32)
                wf[1, pl.ds(0, c_in, stride=2), :] = jnp.zeros((c_in, c_out), jnp.float32)
                wf[1, pl.ds(1, c_in, stride=2), :] = w_v[base].astype(jnp.float32)
                for r in range(2):
                    wl[kd, part * two:(part + 1) * two, r * c_out:(r + 1) * c_out] = wf[r].astype(jnp.bfloat16)
            return carry

        lax.fori_loop(0, 3, step, 0)

    dg_rows = dg_v.reshape(2, 2, rows, two, LANES)

    def dgrad(p, terms, lo, hi):
        def step(k, carry):
            col = pl.multiple_of(k * 2 * LANES, 2 * LANES)
            here = pl.ds(col, 2 * LANES)
            down = pl.ds(pl.multiple_of(col + LANES, LANES), 2 * LANES)
            top, bot = None, None
            for kd, mm in terms:
                o = jnp.dot(wl[kd, :2 * two], mm[:, here], preferred_element_type=jnp.float32)
                d = jnp.dot(wl[kd, 2 * two:], mm[:, down], preferred_element_type=jnp.float32)
                top = o[:two] if top is None else top + o[:two]
                bot = o[two:] + d if bot is None else bot + (o[two:] + d)
            for s, val in ((0, top), (1, bot)):
                for j in range(2):
                    b = 2 * k + j
                    dg_rows[p, s, b] = val[:, j * LANES:(j + 1) * LANES].astype(jnp.bfloat16)
                    pltpu.make_async_copy(dg_v.at[p, s, b], dg_out.at[:, p, s, b], out_sem.at[0]).start()
            return carry

        lax.fori_loop(lo, hi, step, 0)

    class Reduce:
        def __init__(self, idx, r1, r2, r3, own, mid=None):
            self.i, self.r1, self.r2, self.r3, self.own, self.mid = idx, r1, r2, r3, own, mid
            self.base, self.u = groups[idx]
            self.half = self.u * chips
            self.copies = {}

        def off(self, a, b):
            return self.base + a * self.half + b * self.u

        def remote(self, stage, src, dst, dev):
            return pltpu.make_async_remote_copy(
                src_ref=src, dst_ref=dst, send_sem=send_sem.at[self.i, stage - 1],
                recv_sem=recv_sem.at[self.i, stage - 1], device_id=dev, device_id_type=MESH)

        def start(self, stage):
            cps = []
            if stage == 1:
                src = grad.at[pl.ds(self.off(1 - core, 0), self.half)]
                cps.append(self.remote(1, src, self.r1, chip_dev(0, 1 - core)))
            elif stage == 2:
                for k in range(1, chips):
                    src = grad.at[pl.ds(self.off(core, (chip + k) % chips), self.u)]
                    cps.append(self.remote(2, src, self.r2.at[k - 1], chip_dev(k, core)))
            elif stage == 3:
                for k in range(1, chs):
                    if self.mid is None:
                        src, dst = self.r3.at[ch], self.r3.at[ch]
                    else:
                        src, dst = self.mid.at[(ch + k) % chs], self.r3.at[k - 1]
                    cps.append(self.remote(3, src, dst, ch_dev(k)))
            elif stage == 5:
                for k in range(1, chs):
                    cps.append(self.remote(5, self.own.at[ch], self.own.at[ch], ch_dev(k)))
            else:
                own, dst = self.own, wg_out.at[pl.ds(self.off(core, chip), self.u)]
                if self.mid is not None:
                    own = own.reshape(self.u, UNIT, c_out)
                for k in range(1, chips):
                    cps.append(self.remote(4, own, dst, chip_dev(k, core)))
                for k in range(chips):
                    cps.append(self.remote(4, own, dst, chip_dev(k, 1 - core)))
                self.local = pltpu.make_async_copy(own, dst, out_sem.at[1 + self.i])
                self.local.start()
            for c in cps:
                c.start()
            self.copies[stage] = cps

        def finish(self, stage):
            if stage == 1:
                self.copies[1][0].wait()
                s = pl.ds(self.off(core, 0), self.half)
                grad[s] = grad[s] + self.r1[...]
            elif stage == 2:
                whole = pltpu.make_async_remote_copy(
                    src_ref=self.r2, dst_ref=self.r2, send_sem=send_sem.at[self.i, 1],
                    recv_sem=recv_sem.at[self.i, 1], device_id=(sp, ch), device_id_type=MESH)
                whole.wait_send()
                whole.wait_recv()
                v = grad[pl.ds(self.off(core, chip), self.u)]
                for k in range(chips - 1):
                    v = v + self.r2[k]
                if self.mid is None:
                    self.r3[ch] = v
                else:
                    self.mid[...] = v.reshape(self.mid.shape)
            elif stage == 3:
                most = self.r3.at[pl.ds(0, chs - 1)]
                whole = pltpu.make_async_remote_copy(
                    src_ref=most, dst_ref=most, send_sem=send_sem.at[self.i, 2],
                    recv_sem=recv_sem.at[self.i, 2], device_id=(sp, ch), device_id_type=MESH)
                whole.wait_send()
                whole.wait_recv()
                if self.mid is None:
                    v = self.r3[0]
                    for k in range(1, chs):
                        v = v + self.r3[k]
                    self.own[...] = (v * scale).astype(self.own.dtype)
                else:
                    v = self.mid[ch]
                    for k in range(chs - 1):
                        v = v + self.r3[k]
                    self.own[ch] = (v * scale).astype(self.own.dtype)
            elif stage == 5:
                most = self.own.at[pl.ds(0, chs - 1)]
                whole = pltpu.make_async_remote_copy(
                    src_ref=most, dst_ref=most, send_sem=send_sem.at[self.i, 4],
                    recv_sem=recv_sem.at[self.i, 4], device_id=(sp, ch), device_id_type=MESH)
                whole.wait_send()
                whole.wait_recv()
            else:
                most = wg_out.at[pl.ds(self.base, (2 * chips - 1) * self.u)]
                whole = pltpu.make_async_remote_copy(
                    src_ref=most, dst_ref=most, send_sem=send_sem.at[self.i, 3],
                    recv_sem=recv_sem.at[self.i, 3], device_id=(sp, ch), device_id_type=MESH)
                whole.wait_send()
                whole.wait_recv()
                self.local.wait()

    red_a = Reduce(0, r1a, r2a, r3a, own_a, mid_a)
    red_b = Reduce(1, r1b, r2b, r3b, own_b)

    for idx, taps in ((0, 18), (1, 9)):
        lo, hi = groups[idx][0] + taps * ups, groups[idx][0] + groups[idx][1] * 2 * chips
        if lo < hi:
            grad[lo:hi] = jnp.zeros((hi - lo, UNIT, LANES), jnp.float32)

    def halo_done():
        @pl.when(flat > 0)
        def _():
            halo.wait_send()

        @pl.when(flat < last)
        def _():
            halo.wait_recv()

        @pl.when(flat == last)
        def _():
            h_nat[...] = jnp.zeros_like(h_nat)

    half = rows // 2
    both = [(2, mh), (0, mn)]

    wgrad(1, 0, mh)
    wgrad(2, 1, mh)
    red_a.start(1)
    loads[2].wait()
    weights()
    red_a.finish(1)
    red_a.start(2)
    dgrad(0, [(1, mh)], 0, half)
    halo_done()
    spread(h_nat, mn)
    wgrad(0, 1, mn)
    red_b.start(1)
    red_a.finish(2)
    red_a.start(3)
    dgrad(1, both, 0, 1)
    red_b.finish(1)
    red_b.start(2)
    dgrad(1, both, 1, 5)
    red_a.finish(3)
    red_a.start(5)
    red_b.finish(2)
    red_b.start(3)
    dgrad(1, both, 5, half)
    red_a.finish(5)
    red_a.start(4)
    red_b.finish(3)
    red_b.start(4)
    red_a.finish(4)
    red_b.finish(4)
    pltpu.make_async_copy(dg_v, dg_v, out_sem.at[0]).wait()


def store_kernel(groups, ups, dg_in, wg_in, dg_out, wg_out, half_v, wide_v, sem):
    dg_copy = pltpu.make_async_copy(dg_in, dg_out, sem.at[0])
    dg_copy.start()
    load = pltpu.make_async_copy(wg_in, half_v, sem.at[1])
    load.start()
    load.wait()
    outs = []
    for idx, tap0, taps in ((1, 0, 9), (0, 9, 18)):
        here = pl.ds(tap0 * ups, taps * ups)
        wide_v[here] = half_v[pl.ds(groups[idx][0], taps * ups)].astype(jnp.float32)
        outs.append(pltpu.make_async_copy(wide_v.at[here], wg_out.at[here], sem.at[2 + idx]))
        outs[-1].start()
    dg_copy.wait()
    for c in outs:
        c.wait()


def on_device(features, pre_act, cotangent, weight):
    c_in, planes_in, _, _, rows, cols = features.shape
    c_out, planes = pre_act.shape[:2]
    taps = weight.shape[0]
    chips = lax.axis_size("sp") // 2
    chs = lax.axis_size("ch")
    devices = chips * 2 * chs
    scale = 1.0 / math.sqrt(devices * planes * rows * cols)
    ups = c_in // UNIT
    u_a = -(-18 * ups // (2 * chips * chs)) * chs
    u_b = -(-9 * ups // (2 * chips))
    groups = ((u_b * 2 * chips, u_a), (0, u_b))
    units = (u_a + u_b) * 2 * chips
    cfg = (chips, chs, rows, c_in, c_out, scale, groups)
    bf, f32 = jnp.bfloat16, jnp.float32
    span = rows * cols
    any_spec = pl.BlockSpec(memory_space=pl.ANY)

    def part(*lead, dtype=f32):
        return pltpu.VMEM(lead + (UNIT, c_out), dtype)

    held = 2 * units + (u_a + u_b) * (2 * chips + chs)
    vmem = 17 * 2**20 + held * UNIT * c_out * 4
    dg, wg = pl.pallas_call(
        functools.partial(kernel, cfg),
        out_shape=(
            jax.ShapeDtypeStruct((c_in, 2, 2, rows, 2, cols), bf),
            jax.ShapeDtypeStruct((units, UNIT, c_out), bf),
        ),
        in_specs=[pl.BlockSpec(memory_space=pltpu.HBM)] * 4,
        out_specs=(any_spec, any_spec),
        scratch_shapes=[
            pltpu.VMEM((rows, c_out, cols), bf),
            pltpu.VMEM((rows, c_out, cols), bf),
            pltpu.VMEM((2, 2, rows, c_in, 2, cols), bf),
            pltpu.VMEM(weight.shape, bf),
            pltpu.VMEM((rows, c_out, cols), bf),
            pltpu.VMEM((rows, c_out, cols), bf),
            pltpu.VMEM((2 * c_out, span + cols), bf),
            pltpu.VMEM((2 * c_out, span + cols), bf),
            pltpu.VMEM((2, 4 * c_in, span), bf),
            pltpu.VMEM((3, 6 * c_in, 2 * c_out), bf),
            pltpu.VMEM((2, 2 * c_in, c_out), f32),
            pltpu.VMEM((2, 6 * c_in, c_out), f32),
            pltpu.VMEM((2, 2, rows, c_in, 2, cols), bf),
            part(units),
            part(chs, u_a // chs, dtype=bf),
            part(u_b, dtype=bf),
            part(u_a * chips),
            part(u_b * chips),
            part(chips - 1, u_a),
            part(chips - 1, u_b),
            part(chs, u_a // chs),
            part(chs - 1, u_a // chs),
            part(chs, u_b),
            pltpu.SemaphoreType.DMA((4,)),
            pltpu.SemaphoreType.DMA((3,)),
            pltpu.SemaphoreType.DMA,
            pltpu.SemaphoreType.DMA,
            pltpu.SemaphoreType.DMA((2, 5)),
            pltpu.SemaphoreType.DMA((2, 5)),
        ],
        compiler_params=pltpu.CompilerParams(
            collective_id=0, has_side_effects=True, vmem_limit_bytes=vmem
        ),
    )(
        pltpu.with_memory_space_constraint(pre_act.transpose(1, 2, 0, 3), pltpu.HBM),
        pltpu.with_memory_space_constraint(cotangent.transpose(1, 2, 0, 3), pltpu.HBM),
        pltpu.with_memory_space_constraint(features.transpose(0, 1, 2, 4, 3, 5), pltpu.HBM),
        pltpu.with_memory_space_constraint(weight, pltpu.HBM),
    )
    dg, wg = pl.pallas_call(
        functools.partial(store_kernel, groups, ups),
        out_shape=(
            jax.ShapeDtypeStruct((c_in, planes_in, 2, rows, 2, cols), bf),
            jax.ShapeDtypeStruct((taps * ups, UNIT, c_out), f32),
        ),
        in_specs=[any_spec] * 2,
        out_specs=(pl.BlockSpec(memory_space=pltpu.HBM),) * 2,
        scratch_shapes=[
            part(units, dtype=bf),
            part(taps * ups),
            pltpu.SemaphoreType.DMA((4,)),
        ],
        compiler_params=pltpu.CompilerParams(vmem_limit_bytes=2**20 + (units + 2 * taps * ups) * UNIT * c_out * 2),
    )(dg, wg)
    return dg.transpose(0, 1, 2, 4, 3, 5), wg.reshape(taps, c_in, c_out)


def solution(mesh):
    return jax.shard_map(
        on_device,
        mesh=mesh,
        in_specs=(
            P(None, ("sp", "ch"), None, None, None, None),
            P(None, ("sp", "ch"), None, None),
            P(None, ("sp", "ch"), None, None),
            P(),
        ),
        out_specs=(P(None, ("sp", "ch"), None, None, None, None), P()),
        check_vma=False,
    )
```

```python
import functools
import math

import jax
import jax.numpy as jnp
from jax import lax
from jax.experimental import pallas as pl
from jax.experimental.pallas import tpu as pltpu
from jax.sharding import PartitionSpec as P

MESH = pl.DeviceIdType.MESH
LANES = 128
UNIT = 8


def kernel(cfg, pre_hbm, cot_hbm, feat_hbm, w_hbm, dg_out, wg_out, *scr):
    (pre_v, cot_v, feat_v, w_v, m_nat, h_nat, mh, mn, feat_a, wl, wf, ws, dg_v, grad, own_a, own_b, own_c) = scr[:17]
    (r1a, r1d, r2a, r2d, r2b, r2c, mid_a, r3a, r3b, r3c) = scr[17:27]
    in_sem, out_sem, halo_s, halo_r, send_sem, recv_sem = scr[27:]
    chips, chs, rows, c_in, c_out, scale, groups, parts, sub = cfg
    sp = lax.axis_index("sp")
    ch = lax.axis_index("ch")
    chip = sp // 2
    core = sp % 2
    flat = sp * chs + ch
    last = chips * 2 * chs - 1
    span = rows * LANES

    def chip_dev(k, c):
        return (((chip + k) % chips) * 2 + c, ch)

    def ch_dev(k):
        return (sp, (ch + k) % chs)

    bar = pltpu.get_barrier_semaphore()
    prev = jnp.maximum(flat - 1, 0)
    nxt = jnp.minimum(flat + 1, last)

    @pl.when(flat > 0)
    def _():
        pl.semaphore_signal(bar, inc=1, device_id=(prev // chs, prev % chs), device_id_type=MESH)

    @pl.when(flat < last)
    def _():
        pl.semaphore_signal(bar, inc=1, device_id=(nxt // chs, nxt % chs), device_id_type=MESH)

    loads = [
        pltpu.make_async_copy(pre_hbm.at[0], pre_v, in_sem.at[0]),
        pltpu.make_async_copy(cot_hbm.at[0], cot_v, in_sem.at[1]),
        pltpu.make_async_copy(w_hbm, w_v, in_sem.at[2]),
    ]
    loads[0].start()
    loads[1].start()
    for k in range(1, chs):
        pl.semaphore_signal(bar, inc=1, device_id=ch_dev(k), device_id_type=MESH)
    for k in range(1, chips):
        pl.semaphore_signal(bar, inc=1, device_id=chip_dev(k, core), device_id_type=MESH)
    for k in range(chips):
        pl.semaphore_signal(bar, inc=1, device_id=chip_dev(k, 1 - core), device_id_type=MESH)
    loads[2].start()

    def load_feat(k, carry):
        p, s, b = k // (2 * rows), (k // rows) % 2, k % rows
        pltpu.make_async_copy(feat_hbm.at[:, p, s, b], feat_v.at[p, s, b], in_sem.at[3]).start()
        return carry

    lax.fori_loop(0, 4 * rows, load_feat, 0)

    loads[0].wait()
    loads[1].wait()

    def mask_step(b, carry):
        p = pre_v[b].astype(jnp.float32)
        m_nat[b] = jnp.where(p > 0, cot_v[b].astype(jnp.float32), 0.0).astype(jnp.bfloat16)
        return carry

    lax.fori_loop(0, rows, mask_step, 0)
    peers = 2 * chips + chs - 2 + jnp.minimum(flat, 1) + jnp.minimum(last - flat, 1)
    pl.semaphore_wait(bar, peers)

    hc = c_out // 2
    halos = [
        pltpu.make_async_remote_copy(
            src_ref=m_nat.at[:, pl.ds(h * hc, hc)], dst_ref=h_nat.at[:, pl.ds(h * hc, hc)],
            send_sem=halo_s.at[h], recv_sem=halo_r.at[h],
            device_id=(prev // chs, prev % chs), device_id_type=MESH,
        )
        for h in range(2)
    ]

    @pl.when(flat > 0)
    def _():
        halos[0].start()
        halos[1].start()

    lane = lax.broadcasted_iota(jnp.int32, (c_out, LANES), 1)

    def spread(src, dst):
        dst[:, span:] = jnp.zeros((2 * c_out, LANES), jnp.bfloat16)
        for b in range(rows):
            v = src[b]
            dst[:c_out, b * LANES:(b + 1) * LANES] = v
            r = jnp.where(lane == LANES - 1, 0.0, pltpu.roll(v.astype(jnp.float32), LANES - 1, 1))
            dst[c_out:, b * LANES:(b + 1) * LANES] = r.astype(jnp.bfloat16)

    def spread_half(h):
        top, low = 2 * h * hc, (2 * h + 1) * hc
        mn[top:top + c_out, span:] = jnp.zeros((c_out, LANES), jnp.bfloat16)
        for b in range(rows):
            v = h_nat[b, h * hc:(h + 1) * hc]
            mn[top:low, b * LANES:(b + 1) * LANES] = v
            r = jnp.where(lane[:hc] == LANES - 1, 0.0, pltpu.roll(v.astype(jnp.float32), LANES - 1, 1))
            mn[low:low + hc, b * LANES:(b + 1) * LANES] = r.astype(jnp.bfloat16)

    spread(m_nat, mh)
    pltpu.make_async_copy(feat_v, feat_v, in_sem.at[3]).wait()
    two = 2 * c_in

    feat_rows = feat_v.reshape(2, 2, rows, two, LANES)

    def feat_step(k, carry):
        p, s = k // 2, k % 2
        at = pl.ds(pl.multiple_of(s * two, two), two)
        for b in range(rows):
            feat_a[p, at, b * LANES:(b + 1) * LANES] = feat_rows[p, s, b]
        return carry

    lax.fori_loop(0, 4, feat_step, 0)

    ups = c_in // UNIT
    starts = {1: parts[0], 2: parts[1]}

    def put(kd, kh, kw, val):
        base = starts[kd] + (kh * 3 + kw) * ups
        grad[base:base + ups] = val.reshape(ups, UNIT, c_out)

    def wgrad(kd, p, mm):
        dn = (((1,), (1,)), ((), ()))
        o = lax.dot_general(feat_a[p], mm[:, :span], dn, preferred_element_type=jnp.float32)
        d = lax.dot_general(feat_a[p, two:], mm[:, LANES:], dn, preferred_element_type=jnp.float32)
        for r in range(2):
            ws[r, :2 * two] = o[:, r * c_out:(r + 1) * c_out]
            ws[r, 2 * two:] = d[:, r * c_out:(r + 1) * c_out]
        for kh, part in ((1, 0), (2, 1), (0, 2)):
            for kw, r, t in ((1, 0, 0), (2, 0, 1), (0, 1, 1)):
                put(kd, kh, kw, ws[r, pl.ds(part * two + t, c_in, stride=2), :])

    left = lax.broadcasted_iota(jnp.int32, (c_in, c_out), 1) < hc

    def wgrad_half(h):
        dn = (((1,), (1,)), ((), ()))
        at = pl.ds(2 * h * hc, c_out)
        ws[0, :2 * two] = lax.dot_general(feat_a[1], mn[at, :span], dn, preferred_element_type=jnp.float32)
        ws[0, 2 * two:] = lax.dot_general(feat_a[1, two:], mn[at, LANES:], dn, preferred_element_type=jnp.float32)
        even = [ws[0, pl.ds(q * two, c_in, stride=2), :] for q in range(3)]
        odd = [ws[0, pl.ds(q * two + 1, c_in, stride=2), :] for q in range(3)]
        packed = jnp.where(left, even[0], pltpu.roll(even[1], hc, 1))
        for q, val in enumerate(odd + [packed, even[2]]):
            base = groups[1 + h][0] + q * ups
            grad[base:base + ups] = val.reshape(ups, UNIT, c_out)

    def weights():
        def step(kd, carry):
            for part, kh in enumerate((1, 2, 0)):
                base = kd * 9 + kh * 3
                wf[0, pl.ds(0, c_in, stride=2), :] = w_v[base + 1].astype(jnp.float32)
                wf[0, pl.ds(1, c_in, stride=2), :] = w_v[base + 2].astype(jnp.float32)
                wf[1, pl.ds(0, c_in, stride=2), :] = jnp.zeros((c_in, c_out), jnp.float32)
                wf[1, pl.ds(1, c_in, stride=2), :] = w_v[base].astype(jnp.float32)
                a, z = wf[0], wf[1]
                if swap:
                    a, z = jnp.where(wide, a, pltpu.roll(z, hc, 1)), jnp.where(wide, pltpu.roll(a, hc, 1), z)
                wl[kd, part * two:(part + 1) * two, :c_out] = a.astype(jnp.bfloat16)
                wl[kd, part * two:(part + 1) * two, c_out:] = z.astype(jnp.bfloat16)
            return carry

        wide = lax.broadcasted_iota(jnp.int32, (two, c_out), 1) < hc
        swap = True
        step(0, 0)
        swap = False
        lax.fori_loop(1, 3, step, 0)

    dg_rows = dg_v.reshape(2, 2, rows, two, LANES)

    def dgrad(p, terms, lo, hi):
        def step(k, carry):
            col = pl.multiple_of(k * 2 * LANES, 2 * LANES)
            here = pl.ds(col, 2 * LANES)
            down = pl.ds(pl.multiple_of(col + LANES, LANES), 2 * LANES)
            top, bot = None, None
            for kd, mm in terms:
                o = jnp.dot(wl[kd, :2 * two], mm[:, here], preferred_element_type=jnp.float32)
                d = jnp.dot(wl[kd, 2 * two:], mm[:, down], preferred_element_type=jnp.float32)
                top = o[:two] if top is None else top + o[:two]
                bot = o[two:] + d if bot is None else bot + (o[two:] + d)
            for s, val in ((0, top), (1, bot)):
                for j in range(2):
                    b = 2 * k + j
                    dg_rows[p, s, b] = val[:, j * LANES:(j + 1) * LANES].astype(jnp.bfloat16)
                    pltpu.make_async_copy(dg_v.at[p, s, b], dg_out.at[:, p, s, b], out_sem.at[0]).start()
            return carry

        lax.fori_loop(lo, hi, step, 0)

    class Early:
        def __init__(self, i, r1, r2):
            self.i, self.r1, self.r2 = i, r1, r2

        def off(self, a, k):
            return parts[self.i] + (a * chips + k) * sub

        def start(self, stage):
            cps = []
            if stage == 1:
                src = grad.at[pl.ds(self.off(1 - core, 0), sub * chips)]
                cps.append(self.remote(1, src, self.r1, chip_dev(0, 1 - core)))
            else:
                for k in range(1, chips):
                    src = grad.at[pl.ds(self.off(core, (chip + k) % chips), sub)]
                    cps.append(self.remote(2, src, self.r2.at[k - 1], chip_dev(k, core)))
            for c in cps:
                c.start()

        def remote(self, stage, src, dst, dev):
            at = (0, stage - 1 + 6 * self.i) if self.i == 0 else (3, stage - 1)
            return pltpu.make_async_remote_copy(
                src_ref=src, dst_ref=dst, send_sem=send_sem.at[at], recv_sem=recv_sem.at[at],
                device_id=dev, device_id_type=MESH)

        def finish(self, stage):
            buf = self.r1 if stage == 1 else self.r2
            whole = self.remote(stage, buf, buf, (sp, ch))
            whole.wait_send()
            whole.wait_recv()
            if stage == 1:
                s = pl.ds(self.off(core, 0), sub * chips)
                grad[s] = grad[s] + self.r1[...]
            else:
                v = grad[pl.ds(self.off(core, chip), sub)]
                for k in range(chips - 1):
                    v = v + self.r2[k]
                flat_mid = mid_a.reshape(groups[0][1], UNIT, c_out)
                flat_mid[self.i * sub:(self.i + 1) * sub] = v

    class Reduce:
        def __init__(self, idx, r1, r2, r3, own, mid=None):
            self.i, self.r1, self.r2, self.r3, self.own, self.mid = idx, r1, r2, r3, own, mid
            self.base, self.u = groups[idx]
            self.half = self.u * chips
            self.copies = {}

        def off(self, a, b):
            return self.base + a * self.half + b * self.u

        def remote(self, stage, src, dst, dev):
            return pltpu.make_async_remote_copy(
                src_ref=src, dst_ref=dst, send_sem=send_sem.at[self.i, stage - 1],
                recv_sem=recv_sem.at[self.i, stage - 1], device_id=dev, device_id_type=MESH)

        def start(self, stage):
            cps = []
            if stage == 1:
                src = grad.at[pl.ds(self.off(1 - core, 0), self.half)]
                cps.append(self.remote(1, src, self.r1, chip_dev(0, 1 - core)))
            elif stage == 2 and self.r1 is None:
                for j in range(1, 2 * chips):
                    k, c = j // 2, core if j % 2 == 0 else 1 - core
                    src = grad.at[pl.ds(self.off(c, (chip + k) % chips), self.u)]
                    cps.append(self.remote(2, src, self.r2.at[j - 1], chip_dev(k, c)))
            elif stage == 2:
                for k in range(1, chips):
                    src = grad.at[pl.ds(self.off(core, (chip + k) % chips), self.u)]
                    cps.append(self.remote(2, src, self.r2.at[k - 1], chip_dev(k, core)))
            elif stage == 3:
                for k in range(1, chs):
                    if self.mid is None:
                        src, dst = self.r3.at[ch], self.r3.at[ch]
                    else:
                        src, dst = self.mid.at[(ch + k) % chs], self.r3.at[k - 1]
                    cps.append(self.remote(3, src, dst, ch_dev(k)))
            elif stage == 6:
                ref = wg_out.at[pl.ds(self.off(core, 0), self.half)]
                cps.append(self.remote(6, ref, ref, chip_dev(0, 1 - core)))
            elif stage == 5:
                for k in range(1, chs):
                    cps.append(self.remote(5, self.own.at[ch], self.own.at[ch], ch_dev(k)))
            else:
                own, dst = self.own, wg_out.at[pl.ds(self.off(core, chip), self.u)]
                if self.mid is not None:
                    own = own.reshape(self.u, UNIT, c_out)
                for k in range(1, chips):
                    cps.append(self.remote(4, own, dst, chip_dev(k, core)))
                for k in range(chips if self.r1 is None else 0):
                    cps.append(self.remote(4, own, dst, chip_dev(k, 1 - core)))
                self.local = pltpu.make_async_copy(own, dst, out_sem.at[1 + self.i])
                self.local.start()
            for c in cps:
                c.start()
            self.copies[stage] = cps

        def finish(self, stage):
            if stage == 1:
                self.copies[1][0].wait()
                s = pl.ds(self.off(core, 0), self.half)
                grad[s] = grad[s] + self.r1[...]
            elif stage == 2:
                whole = pltpu.make_async_remote_copy(
                    src_ref=self.r2, dst_ref=self.r2, send_sem=send_sem.at[self.i, 1],
                    recv_sem=recv_sem.at[self.i, 1], device_id=(sp, ch), device_id_type=MESH)
                whole.wait_send()
                whole.wait_recv()
                v = grad[pl.ds(self.off(core, chip), self.u)]
                for k in range(self.r2.shape[0]):
                    v = v + self.r2[k]
                if self.mid is None:
                    self.r3[ch] = v
                else:
                    self.mid[...] = v.reshape(self.mid.shape)
            elif stage == 3:
                most = self.r3.at[pl.ds(0, chs - 1)]
                whole = pltpu.make_async_remote_copy(
                    src_ref=most, dst_ref=most, send_sem=send_sem.at[self.i, 2],
                    recv_sem=recv_sem.at[self.i, 2], device_id=(sp, ch), device_id_type=MESH)
                whole.wait_send()
                whole.wait_recv()
                if self.mid is None:
                    v = self.r3[0]
                    for k in range(1, chs):
                        v = v + self.r3[k]
                    self.own[...] = (v * scale).astype(self.own.dtype)
                else:
                    v = self.mid[ch]
                    for k in range(chs - 1):
                        v = v + self.r3[k]
                    self.own[ch] = (v * scale).astype(self.own.dtype)
            elif stage == 5:
                most = self.own.at[pl.ds(0, chs - 1)]
                whole = pltpu.make_async_remote_copy(
                    src_ref=most, dst_ref=most, send_sem=send_sem.at[self.i, 4],
                    recv_sem=recv_sem.at[self.i, 4], device_id=(sp, ch), device_id_type=MESH)
                whole.wait_send()
                whole.wait_recv()
            elif stage == 6:
                self.copies[6][0].wait()
            else:
                others = 2 * chips - 1 if self.r1 is None else chips - 1
                most = wg_out.at[pl.ds(self.base, others * self.u)]
                whole = pltpu.make_async_remote_copy(
                    src_ref=most, dst_ref=most, send_sem=send_sem.at[self.i, 3],
                    recv_sem=recv_sem.at[self.i, 3], device_id=(sp, ch), device_id_type=MESH)
                whole.wait_send()
                whole.wait_recv()
                self.local.wait()

    red_a = Reduce(0, r1a, None, r3a, own_a, mid_a)
    early = [Early(0, r1a, r2a), Early(1, r1d, r2d)]
    red_b = Reduce(1, None, r2b, r3b, own_b)
    red_c = Reduce(2, None, r2c, r3c, own_c)

    for lo, count, room in (
        (parts[0], 9 * ups, sub * 2 * chips),
        (parts[1], 9 * ups, sub * 2 * chips),
        (groups[1][0], 5 * ups, groups[1][1] * 2 * chips),
        (groups[2][0], 5 * ups, groups[2][1] * 2 * chips),
    ):
        if count < room:
            grad[lo + count:lo + room] = jnp.zeros((room - count, UNIT, LANES), jnp.float32)
    if 2 * sub < groups[0][1]:
        rest = mid_a.reshape(groups[0][1], UNIT, c_out)
        rest[2 * sub:] = jnp.zeros((groups[0][1] - 2 * sub, UNIT, LANES), jnp.float32)

    def halo_done(h):
        @pl.when(flat > 0)
        def _():
            halos[h].wait_send()

        @pl.when(flat < last)
        def _():
            halos[h].wait_recv()

        @pl.when(flat == last)
        def _():
            h_nat[:, h * hc:(h + 1) * hc] = jnp.zeros((rows, hc, LANES), jnp.bfloat16)

    half = rows // 2
    both = [(2, mh), (0, mn)]

    wgrad(1, 0, mh)
    early[0].start(1)
    wgrad(2, 1, mh)
    early[1].start(1)
    early[0].finish(1)
    early[0].start(2)
    loads[2].wait()
    weights()
    early[1].finish(1)
    early[1].start(2)
    dgrad(0, [(1, mh)], 0, half)
    early[0].finish(2)
    halo_done(0)
    spread_half(0)
    wgrad_half(0)
    red_b.start(2)

    early[1].finish(2)
    red_a.start(3)
    halo_done(1)
    spread_half(1)
    wgrad_half(1)
    red_c.start(2)
    red_a.finish(3)
    red_a.start(5)
    red_b.finish(2)
    red_b.start(3)
    dgrad(1, both, 0, 4)
    red_c.finish(2)
    red_c.start(3)
    red_a.finish(5)
    red_a.start(4)
    dgrad(1, both, 4, half)
    red_b.finish(3)
    red_b.start(4)
    red_c.finish(3)
    red_c.start(4)
    red_a.finish(4)
    red_a.start(6)
    red_a.finish(6)
    red_b.finish(4)
    red_c.finish(4)
    pltpu.make_async_copy(dg_v, dg_v, out_sem.at[0]).wait()


def store_kernel(groups, sub, ups, dg_in, wg_in, dg_out, wg_out, half_v, wide_v, sem):
    dg_copy = pltpu.make_async_copy(dg_in, dg_out, sem.at[0])
    dg_copy.start()
    load = pltpu.make_async_copy(wg_in, half_v, sem.at[1])
    load.start()
    load.wait()
    outs = []

    def send(tap0, taps, slot):
        here = pl.ds(tap0 * ups, taps * ups)
        outs.append(pltpu.make_async_copy(wide_v.at[here], wg_out.at[here], sem.at[slot]))
        outs[-1].start()

    for i in range(2):
        for j in range(-(-9 * ups // sub)):
            n = min(sub, 9 * ups - j * sub)
            src = groups[0][0] + j * groups[0][1] + i * sub
            wide_v[pl.ds(9 * (i + 1) * ups + j * sub, n)] = half_v[pl.ds(src, n)].astype(jnp.float32)
    send(9, 18, 2)
    lanes = half_v.shape[2]
    left = lax.broadcasted_iota(jnp.int32, (ups * UNIT, lanes), 1) < lanes // 2

    def block(h, q):
        v = half_v[pl.ds(groups[1 + h][0] + q * ups, ups)].astype(jnp.float32)
        return v.reshape(ups * UNIT, lanes)

    def put(tap, low, high):
        wide_v[pl.ds(tap * ups, ups)] = jnp.where(left, low, high).reshape(ups, UNIT, lanes)

    def other(v):
        return pltpu.roll(v, lanes // 2, 1)

    for q, kh in enumerate((1, 2, 0)):
        put(kh * 3 + 2, block(0, q), other(block(1, q)))
        put(kh * 3, other(block(0, q)), block(1, q))
    put(4, block(0, 3), other(block(1, 3)))
    put(7, other(block(0, 3)), block(1, 3))
    put(1, block(0, 4), other(block(1, 4)))
    send(0, 9, 3)
    dg_copy.wait()
    for c in outs:
        c.wait()


def on_device(features, pre_act, cotangent, weight):
    c_in, planes_in, _, _, rows, cols = features.shape
    c_out, planes = pre_act.shape[:2]
    taps = weight.shape[0]
    chips = lax.axis_size("sp") // 2
    chs = lax.axis_size("ch")
    devices = chips * 2 * chs
    scale = 1.0 / math.sqrt(devices * planes * rows * cols)
    ups = c_in // UNIT
    sub = -(-9 * ups // (2 * chips))
    u_a = -(-2 * sub // chs) * chs
    u_b = -(-5 * ups // (2 * chips))
    span_b = u_b * 2 * chips
    groups = ((2 * span_b, u_a), (0, u_b), (span_b, u_b))
    units = u_a * 2 * chips + 2 * span_b
    parts = (2 * span_b, 2 * span_b + sub * 2 * chips)
    cfg = (chips, chs, rows, c_in, c_out, scale, groups, parts, sub)
    bf, f32 = jnp.bfloat16, jnp.float32
    span = rows * cols
    any_spec = pl.BlockSpec(memory_space=pl.ANY)

    def part(*lead, dtype=f32):
        return pltpu.VMEM(lead + (UNIT, c_out), dtype)

    held = 2 * units + (u_a + 2 * u_b) * (2 * chips + chs)
    vmem = 17 * 2**20 + held * UNIT * c_out * 4
    dg, wg = pl.pallas_call(
        functools.partial(kernel, cfg),
        out_shape=(
            jax.ShapeDtypeStruct((c_in, 2, 2, rows, 2, cols), bf),
            jax.ShapeDtypeStruct((units, UNIT, c_out), bf),
        ),
        in_specs=[pl.BlockSpec(memory_space=pltpu.HBM)] * 4,
        out_specs=(any_spec, any_spec),
        scratch_shapes=[
            pltpu.VMEM((rows, c_out, cols), bf),
            pltpu.VMEM((rows, c_out, cols), bf),
            pltpu.VMEM((2, 2, rows, c_in, 2, cols), bf),
            pltpu.VMEM(weight.shape, bf),
            pltpu.VMEM((rows, c_out, cols), bf),
            pltpu.VMEM((rows, c_out, cols), bf),
            pltpu.VMEM((2 * c_out, span + cols), bf),
            pltpu.VMEM((2 * c_out, span + cols), bf),
            pltpu.VMEM((2, 4 * c_in, span), bf),
            pltpu.VMEM((3, 6 * c_in, 2 * c_out), bf),
            pltpu.VMEM((2, 2 * c_in, c_out), f32),
            pltpu.VMEM((2, 6 * c_in, c_out), f32),
            pltpu.VMEM((2, 2, rows, c_in, 2, cols), bf),
            part(units),
            part(chs, u_a // chs, dtype=bf),
            part(u_b, dtype=bf),
            part(u_b, dtype=bf),
            part(sub * chips),
            part(sub * chips),
            part(chips - 1, sub),
            part(chips - 1, sub),
            part(2 * chips - 1, u_b),
            part(2 * chips - 1, u_b),
            part(chs, u_a // chs),
            part(chs - 1, u_a // chs),
            part(chs, u_b),
            part(chs, u_b),
            pltpu.SemaphoreType.DMA((4,)),
            pltpu.SemaphoreType.DMA((4,)),
            pltpu.SemaphoreType.DMA((2,)),
            pltpu.SemaphoreType.DMA((2,)),
            pltpu.SemaphoreType.DMA((4, 6)),
            pltpu.SemaphoreType.DMA((4, 6)),
        ],
        compiler_params=pltpu.CompilerParams(
            collective_id=0, has_side_effects=True, vmem_limit_bytes=vmem
        ),
    )(
        pltpu.with_memory_space_constraint(pre_act.transpose(1, 2, 0, 3), pltpu.HBM),
        pltpu.with_memory_space_constraint(cotangent.transpose(1, 2, 0, 3), pltpu.HBM),
        pltpu.with_memory_space_constraint(features.transpose(0, 1, 2, 4, 3, 5), pltpu.HBM),
        pltpu.with_memory_space_constraint(weight, pltpu.HBM),
    )
    dg, wg = pl.pallas_call(
        functools.partial(store_kernel, groups, sub, ups),
        out_shape=(
            jax.ShapeDtypeStruct((c_in, planes_in, 2, rows, 2, cols), bf),
            jax.ShapeDtypeStruct((taps * ups, UNIT, c_out), f32),
        ),
        in_specs=[any_spec] * 2,
        out_specs=(pl.BlockSpec(memory_space=pltpu.HBM),) * 2,
        scratch_shapes=[
            part(units, dtype=bf),
            part(taps * ups),
            pltpu.SemaphoreType.DMA((4,)),
        ],
        compiler_params=pltpu.CompilerParams(vmem_limit_bytes=2**20 + (units + 2 * taps * ups) * UNIT * c_out * 2),
    )(dg, wg)
    return dg.transpose(0, 1, 2, 4, 3, 5), wg.reshape(taps, c_in, c_out)


def solution(mesh):
    return jax.shard_map(
        on_device,
        mesh=mesh,
        in_specs=(
            P(None, ("sp", "ch"), None, None, None, None),
            P(None, ("sp", "ch"), None, None),
            P(None, ("sp", "ch"), None, None),
            P(),
        ),
        out_specs=(P(None, ("sp", "ch"), None, None, None, None), P()),
        check_vma=False,
    )
```

```python
import functools
import math

import jax
import jax.numpy as jnp
from jax import lax
from jax.experimental import pallas as pl
from jax.experimental.pallas import tpu as pltpu
from jax.sharding import PartitionSpec as P

MESH = pl.DeviceIdType.MESH
LANES = 128
UNIT = 8


def kernel(cfg, pre_hbm, cot_hbm, feat_hbm, w_hbm, dg_out, wg_out, *scr):
    (pre_v, cot_v, feat_v, w_v, m_nat, h_nat, mh, mn, feat_a, wl, wf, ws, dg_v, grad, own_a, own_b, own_c) = scr[:17]
    (r1a, r1d, r2a, r2d, r2b, r2c, mid_a, r3a, r3b, r3c) = scr[17:27]
    relay_v, in_sem, out_sem, halo_s, halo_r, relay_s, relay_r, send_sem, recv_sem = scr[27:]
    chips, chs, rows, c_in, c_out, scale, groups, parts, sub = cfg
    sp = lax.axis_index("sp")
    ch = lax.axis_index("ch")
    chip = sp // 2
    core = sp % 2
    flat = sp * chs + ch
    last = chips * 2 * chs - 1
    span = rows * LANES

    def chip_dev(k, c):
        return (((chip + k) % chips) * 2 + c, ch)

    def ch_dev(k):
        return (sp, (ch + k) % chs)

    bar = pltpu.get_barrier_semaphore()
    prev = jnp.maximum(flat - 1, 0)
    nxt = jnp.minimum(flat + 1, last)

    @pl.when(flat > 0)
    def _():
        pl.semaphore_signal(bar, inc=1, device_id=(prev // chs, prev % chs), device_id_type=MESH)

    @pl.when(flat < last)
    def _():
        pl.semaphore_signal(bar, inc=1, device_id=(nxt // chs, nxt % chs), device_id_type=MESH)

    loads = [
        pltpu.make_async_copy(pre_hbm.at[0], pre_v, in_sem.at[0]),
        pltpu.make_async_copy(cot_hbm.at[0], cot_v, in_sem.at[1]),
        pltpu.make_async_copy(w_hbm, w_v, in_sem.at[2]),
    ]
    loads[0].start()
    loads[1].start()
    for k in range(1, chs):
        pl.semaphore_signal(bar, inc=1, device_id=ch_dev(k), device_id_type=MESH)
    for k in range(1, chips):
        pl.semaphore_signal(bar, inc=1, device_id=chip_dev(k, core), device_id_type=MESH)
    for k in range(chips):
        pl.semaphore_signal(bar, inc=1, device_id=chip_dev(k, 1 - core), device_id_type=MESH)
    loads[2].start()

    def load_feat(k, carry):
        p, s, b = k // (2 * rows), (k // rows) % 2, k % rows
        pltpu.make_async_copy(feat_hbm.at[:, p, s, b], feat_v.at[p, s, b], in_sem.at[3]).start()
        return carry

    lax.fori_loop(0, 4 * rows, load_feat, 0)

    loads[0].wait()
    loads[1].wait()

    def mask_step(b, carry):
        p = pre_v[b].astype(jnp.float32)
        m_nat[b] = jnp.where(p > 0, cot_v[b].astype(jnp.float32), 0.0).astype(jnp.bfloat16)
        return carry

    lax.fori_loop(0, rows, mask_step, 0)
    peers = 2 * chips + chs - 2 + jnp.minimum(flat, 1) + jnp.minimum(last - flat, 1)
    pl.semaphore_wait(bar, peers)

    hc = c_out // 2
    halos = [
        pltpu.make_async_remote_copy(
            src_ref=m_nat.at[:, pl.ds(h * hc, hc)], dst_ref=h_nat.at[:, pl.ds(h * hc, hc)],
            send_sem=halo_s.at[h], recv_sem=halo_r.at[h],
            device_id=(prev // chs, prev % chs), device_id_type=MESH,
        )
        for h in range(2)
    ]

    wrap = jnp.logical_and(core == 0, ch == 0) if chs > 1 else False

    @pl.when(jnp.logical_and(flat > 0, jnp.logical_not(wrap)))
    def _():
        halos[0].start()
        halos[1].start()

    def piece(h, lo, hi):
        return m_nat.at[pl.ds(lo, hi - lo), pl.ds(h * hc, hc)]

    def landing(h, lo, hi):
        return h_nat.at[pl.ds(lo, hi - lo), pl.ds(h * hc, hc)]

    def share(c):
        total = 1 * 2 * rows * (chips - c) // (chips * 2)
        return min(rows, total), max(0, total - rows)

    def send_wrap(c):
        ones, zeros = share(c)
        to, via = (2 * c - 1, chs - 1), (2 * c - 1, 0)
        for h, lo, hi, at in (
            (1, 0, ones, 0), (0, 0, zeros, ones), (0, zeros, rows, None), (1, ones, rows, None),
        ):
            if lo < hi:
                direct = at is None
                pltpu.make_async_remote_copy(
                    src_ref=piece(h, lo, hi),
                    dst_ref=landing(h, lo, hi) if direct else relay_v.at[pl.ds(at, hi - lo)],
                    send_sem=halo_s.at[h], recv_sem=halo_r.at[h] if direct else relay_r,
                    device_id=to if direct else via, device_id_type=MESH,
                ).start()

    for c in range(1, chips):
        if chs > 1:

            @pl.when(jnp.logical_and(wrap, chip == c))
            def _(c=c):
                send_wrap(c)

    def forwards(c):
        ones, zeros = share(c)
        return [
            pltpu.make_async_remote_copy(
                src_ref=relay_v.at[pl.ds(at, n)], dst_ref=landing(h, 0, n),
                send_sem=relay_s.at[h], recv_sem=halo_r.at[h],
                device_id=(sp, chs - 1), device_id_type=MESH,
            )
            for h, n, at in ((1, ones, 0), (0, zeros, ones))
            if n
        ]

    def at_relay(c):
        return jnp.logical_and(jnp.logical_and(core == 1, ch == 0), chip == c - 1)

    def relay():
        for c in range(1, chips if chs > 1 else 1):
            whole = relay_v.at[pl.ds(0, sum(share(c)))]

            @pl.when(at_relay(c))
            def _(c=c, whole=whole):
                pltpu.make_async_remote_copy(
                    src_ref=whole, dst_ref=whole, send_sem=relay_s.at[0], recv_sem=relay_r,
                    device_id=(sp, ch), device_id_type=MESH).wait_recv()
                for f in forwards(c):
                    f.start()

    def relay_done():
        for c in range(1, chips if chs > 1 else 1):

            @pl.when(at_relay(c))
            def _(c=c):
                for f in forwards(c):
                    f.wait_send()

    lane = lax.broadcasted_iota(jnp.int32, (c_out, LANES), 1)

    def spread(src, dst):
        dst[:, span:] = jnp.zeros((2 * c_out, LANES), jnp.bfloat16)
        for b in range(rows):
            v = src[b]
            dst[:c_out, b * LANES:(b + 1) * LANES] = v
            r = jnp.where(lane == LANES - 1, 0.0, pltpu.roll(v.astype(jnp.float32), LANES - 1, 1))
            dst[c_out:, b * LANES:(b + 1) * LANES] = r.astype(jnp.bfloat16)

    def spread_half(h):
        top, low = 2 * h * hc, (2 * h + 1) * hc
        mn[top:top + c_out, span:] = jnp.zeros((c_out, LANES), jnp.bfloat16)
        for b in range(rows):
            v = h_nat[b, h * hc:(h + 1) * hc]
            mn[top:low, b * LANES:(b + 1) * LANES] = v
            r = jnp.where(lane[:hc] == LANES - 1, 0.0, pltpu.roll(v.astype(jnp.float32), LANES - 1, 1))
            mn[low:low + hc, b * LANES:(b + 1) * LANES] = r.astype(jnp.bfloat16)

    spread(m_nat, mh)
    pltpu.make_async_copy(feat_v, feat_v, in_sem.at[3]).wait()
    two = 2 * c_in

    feat_rows = feat_v.reshape(2, 2, rows, two, LANES)

    def feat_step(k, carry):
        p, s = k // 2, k % 2
        at = pl.ds(pl.multiple_of(s * two, two), two)
        for b in range(rows):
            feat_a[p, at, b * LANES:(b + 1) * LANES] = feat_rows[p, s, b]
        return carry

    lax.fori_loop(0, 4, feat_step, 0)

    ups = c_in // UNIT
    starts = {1: parts[0], 2: parts[1]}

    def put(kd, kh, kw, val):
        base = starts[kd] + (kh * 3 + kw) * ups
        grad[base:base + ups] = val.reshape(ups, UNIT, c_out)

    def wgrad(kd, p, mm):
        dn = (((1,), (1,)), ((), ()))
        o = lax.dot_general(feat_a[p], mm[:, :span], dn, preferred_element_type=jnp.float32)
        d = lax.dot_general(feat_a[p, two:], mm[:, LANES:], dn, preferred_element_type=jnp.float32)
        for r in range(2):
            ws[r, :2 * two] = o[:, r * c_out:(r + 1) * c_out]
            ws[r, 2 * two:] = d[:, r * c_out:(r + 1) * c_out]
        for kh, part in ((1, 0), (2, 1), (0, 2)):
            for kw, r, t in ((1, 0, 0), (2, 0, 1), (0, 1, 1)):
                put(kd, kh, kw, ws[r, pl.ds(part * two + t, c_in, stride=2), :])

    left = lax.broadcasted_iota(jnp.int32, (c_in, c_out), 1) < hc

    def wgrad_half(h):
        dn = (((1,), (1,)), ((), ()))
        at = pl.ds(2 * h * hc, c_out)
        ws[0, :2 * two] = lax.dot_general(feat_a[1], mn[at, :span], dn, preferred_element_type=jnp.float32)
        ws[0, 2 * two:] = lax.dot_general(feat_a[1, two:], mn[at, LANES:], dn, preferred_element_type=jnp.float32)
        even = [ws[0, pl.ds(q * two, c_in, stride=2), :] for q in range(3)]
        odd = [ws[0, pl.ds(q * two + 1, c_in, stride=2), :] for q in range(3)]
        packed = jnp.where(left, even[0], pltpu.roll(even[1], hc, 1))
        for q, val in enumerate(odd + [packed, even[2]]):
            base = groups[1 + h][0] + q * ups
            grad[base:base + ups] = val.reshape(ups, UNIT, c_out)

    def weights():
        def step(kd, carry):
            for part, kh in enumerate((1, 2, 0)):
                base = kd * 9 + kh * 3
                wf[0, pl.ds(0, c_in, stride=2), :] = w_v[base + 1].astype(jnp.float32)
                wf[0, pl.ds(1, c_in, stride=2), :] = w_v[base + 2].astype(jnp.float32)
                wf[1, pl.ds(0, c_in, stride=2), :] = jnp.zeros((c_in, c_out), jnp.float32)
                wf[1, pl.ds(1, c_in, stride=2), :] = w_v[base].astype(jnp.float32)
                a, z = wf[0], wf[1]
                if swap:
                    a, z = jnp.where(wide, a, pltpu.roll(z, hc, 1)), jnp.where(wide, pltpu.roll(a, hc, 1), z)
                wl[kd, part * two:(part + 1) * two, :c_out] = a.astype(jnp.bfloat16)
                wl[kd, part * two:(part + 1) * two, c_out:] = z.astype(jnp.bfloat16)
            return carry

        wide = lax.broadcasted_iota(jnp.int32, (two, c_out), 1) < hc
        swap = True
        step(0, 0)
        swap = False
        lax.fori_loop(1, 3, step, 0)

    dg_rows = dg_v.reshape(2, 2, rows, two, LANES)

    def dgrad(p, terms, lo, hi):
        def step(k, carry):
            col = pl.multiple_of(k * 2 * LANES, 2 * LANES)
            here = pl.ds(col, 2 * LANES)
            down = pl.ds(pl.multiple_of(col + LANES, LANES), 2 * LANES)
            top, bot = None, None
            for kd, mm in terms:
                o = jnp.dot(wl[kd, :2 * two], mm[:, here], preferred_element_type=jnp.float32)
                d = jnp.dot(wl[kd, 2 * two:], mm[:, down], preferred_element_type=jnp.float32)
                top = o[:two] if top is None else top + o[:two]
                bot = o[two:] + d if bot is None else bot + (o[two:] + d)
            for s, val in ((0, top), (1, bot)):
                for j in range(2):
                    b = 2 * k + j
                    dg_rows[p, s, b] = val[:, j * LANES:(j + 1) * LANES].astype(jnp.bfloat16)
                    pltpu.make_async_copy(dg_v.at[p, s, b], dg_out.at[:, p, s, b], out_sem.at[0]).start()
            return carry

        lax.fori_loop(lo, hi, step, 0)

    class Early:
        def __init__(self, i, r1, r2):
            self.i, self.r1, self.r2 = i, r1, r2

        def off(self, a, k):
            return parts[self.i] + (a * chips + k) * sub

        def start(self, stage):
            cps = []
            if stage == 1:
                src = grad.at[pl.ds(self.off(1 - core, 0), sub * chips)]
                cps.append(self.remote(1, src, self.r1, chip_dev(0, 1 - core)))
            else:
                for k in range(1, chips):
                    src = grad.at[pl.ds(self.off(core, (chip + k) % chips), sub)]
                    cps.append(self.remote(2, src, self.r2.at[k - 1], chip_dev(k, core)))
            for c in cps:
                c.start()

        def remote(self, stage, src, dst, dev):
            at = (0, stage - 1 + 6 * self.i) if self.i == 0 else (3, stage - 1)
            return pltpu.make_async_remote_copy(
                src_ref=src, dst_ref=dst, send_sem=send_sem.at[at], recv_sem=recv_sem.at[at],
                device_id=dev, device_id_type=MESH)

        def finish(self, stage):
            buf = self.r1 if stage == 1 else self.r2
            whole = self.remote(stage, buf, buf, (sp, ch))
            whole.wait_send()
            whole.wait_recv()
            if stage == 1:
                s = pl.ds(self.off(core, 0), sub * chips)
                grad[s] = grad[s] + self.r1[...]
            else:
                v = grad[pl.ds(self.off(core, chip), sub)]
                for k in range(chips - 1):
                    v = v + self.r2[k]
                flat_mid = mid_a.reshape(groups[0][1], UNIT, c_out)
                flat_mid[self.i * sub:(self.i + 1) * sub] = v

    class Reduce:
        def __init__(self, idx, r1, r2, r3, own, mid=None):
            self.i, self.r1, self.r2, self.r3, self.own, self.mid = idx, r1, r2, r3, own, mid
            self.base, self.u = groups[idx]
            self.half = self.u * chips
            self.copies = {}

        def off(self, a, b):
            return self.base + a * self.half + b * self.u

        def remote(self, stage, src, dst, dev):
            return pltpu.make_async_remote_copy(
                src_ref=src, dst_ref=dst, send_sem=send_sem.at[self.i, stage - 1],
                recv_sem=recv_sem.at[self.i, stage - 1], device_id=dev, device_id_type=MESH)

        def start(self, stage):
            cps = []
            if stage == 1:
                src = grad.at[pl.ds(self.off(1 - core, 0), self.half)]
                cps.append(self.remote(1, src, self.r1, chip_dev(0, 1 - core)))
            elif stage == 2 and self.r1 is None:
                for j in range(1, 2 * chips):
                    k, c = j // 2, core if j % 2 == 0 else 1 - core
                    src = grad.at[pl.ds(self.off(c, (chip + k) % chips), self.u)]
                    cps.append(self.remote(2, src, self.r2.at[j - 1], chip_dev(k, c)))
            elif stage == 2:
                for k in range(1, chips):
                    src = grad.at[pl.ds(self.off(core, (chip + k) % chips), self.u)]
                    cps.append(self.remote(2, src, self.r2.at[k - 1], chip_dev(k, core)))
            elif stage == 3:
                for k in range(1, chs):
                    if self.mid is None:
                        src, dst = self.r3.at[ch], self.r3.at[ch]
                    else:
                        src, dst = self.mid.at[(ch + k) % chs], self.r3.at[k - 1]
                    cps.append(self.remote(3, src, dst, ch_dev(k)))
            elif stage == 6:
                ref = wg_out.at[pl.ds(self.off(core, 0), self.half)]
                cps.append(self.remote(6, ref, ref, chip_dev(0, 1 - core)))
            elif stage == 5:
                for k in range(1, chs):
                    cps.append(self.remote(5, self.own.at[ch], self.own.at[ch], ch_dev(k)))
            else:
                own, dst = self.own, wg_out.at[pl.ds(self.off(core, chip), self.u)]
                if self.mid is not None:
                    own = own.reshape(self.u, UNIT, c_out)
                for k in range(1, chips):
                    cps.append(self.remote(4, own, dst, chip_dev(k, core)))
                for k in range(chips if self.r1 is None else 0):
                    cps.append(self.remote(4, own, dst, chip_dev(k, 1 - core)))
                self.local = pltpu.make_async_copy(own, dst, out_sem.at[1 + self.i])
                self.local.start()
            for c in cps:
                c.start()
            self.copies[stage] = cps

        def finish(self, stage):
            if stage == 1:
                self.copies[1][0].wait()
                s = pl.ds(self.off(core, 0), self.half)
                grad[s] = grad[s] + self.r1[...]
            elif stage == 2:
                whole = pltpu.make_async_remote_copy(
                    src_ref=self.r2, dst_ref=self.r2, send_sem=send_sem.at[self.i, 1],
                    recv_sem=recv_sem.at[self.i, 1], device_id=(sp, ch), device_id_type=MESH)
                whole.wait_send()
                whole.wait_recv()
                v = grad[pl.ds(self.off(core, chip), self.u)]
                for k in range(self.r2.shape[0]):
                    v = v + self.r2[k]
                if self.mid is None:
                    self.r3[ch] = v
                else:
                    self.mid[...] = v.reshape(self.mid.shape)
            elif stage == 3:
                most = self.r3.at[pl.ds(0, chs - 1)]
                whole = pltpu.make_async_remote_copy(
                    src_ref=most, dst_ref=most, send_sem=send_sem.at[self.i, 2],
                    recv_sem=recv_sem.at[self.i, 2], device_id=(sp, ch), device_id_type=MESH)
                whole.wait_send()
                whole.wait_recv()
                if self.mid is None:
                    v = self.r3[0]
                    for k in range(1, chs):
                        v = v + self.r3[k]
                    self.own[...] = (v * scale).astype(self.own.dtype)
                else:
                    v = self.mid[ch]
                    for k in range(chs - 1):
                        v = v + self.r3[k]
                    self.own[ch] = (v * scale).astype(self.own.dtype)
            elif stage == 5:
                most = self.own.at[pl.ds(0, chs - 1)]
                whole = pltpu.make_async_remote_copy(
                    src_ref=most, dst_ref=most, send_sem=send_sem.at[self.i, 4],
                    recv_sem=recv_sem.at[self.i, 4], device_id=(sp, ch), device_id_type=MESH)
                whole.wait_send()
                whole.wait_recv()
            elif stage == 6:
                self.copies[6][0].wait()
            else:
                others = 2 * chips - 1 if self.r1 is None else chips - 1
                most = wg_out.at[pl.ds(self.base, others * self.u)]
                whole = pltpu.make_async_remote_copy(
                    src_ref=most, dst_ref=most, send_sem=send_sem.at[self.i, 3],
                    recv_sem=recv_sem.at[self.i, 3], device_id=(sp, ch), device_id_type=MESH)
                whole.wait_send()
                whole.wait_recv()
                self.local.wait()

    red_a = Reduce(0, r1a, None, r3a, own_a, mid_a)
    early = [Early(0, r1a, r2a), Early(1, r1d, r2d)]
    red_b = Reduce(1, None, r2b, r3b, own_b)
    red_c = Reduce(2, None, r2c, r3c, own_c)

    for lo, count, room in (
        (parts[0], 9 * ups, sub * 2 * chips),
        (parts[1], 9 * ups, sub * 2 * chips),
        (groups[1][0], 5 * ups, groups[1][1] * 2 * chips),
        (groups[2][0], 5 * ups, groups[2][1] * 2 * chips),
    ):
        if count < room:
            grad[lo + count:lo + room] = jnp.zeros((room - count, UNIT, LANES), jnp.float32)
    if 2 * sub < groups[0][1]:
        rest = mid_a.reshape(groups[0][1], UNIT, c_out)
        rest[2 * sub:] = jnp.zeros((groups[0][1] - 2 * sub, UNIT, LANES), jnp.float32)

    def halo_done(h):
        @pl.when(flat > 0)
        def _():
            halos[h].wait_send()

        @pl.when(flat < last)
        def _():
            halos[h].wait_recv()

        @pl.when(flat == last)
        def _():
            h_nat[:, h * hc:(h + 1) * hc] = jnp.zeros((rows, hc, LANES), jnp.bfloat16)

    half = rows // 2
    both = [(2, mh), (0, mn)]

    wgrad(1, 0, mh)
    early[0].start(1)
    wgrad(2, 1, mh)
    early[1].start(1)
    early[0].finish(1)
    early[0].start(2)
    loads[2].wait()
    weights()
    early[1].finish(1)
    early[1].start(2)
    dgrad(0, [(1, mh)], 0, half)
    relay()
    early[0].finish(2)
    halo_done(0)
    spread_half(0)
    wgrad_half(0)
    red_b.start(2)

    early[1].finish(2)
    red_a.start(3)
    halo_done(1)
    spread_half(1)
    wgrad_half(1)
    red_c.start(2)
    red_a.finish(3)
    red_a.start(5)
    red_b.finish(2)
    red_b.start(3)
    dgrad(1, both, 0, 4)
    red_c.finish(2)
    red_c.start(3)
    red_a.finish(5)
    red_a.start(4)
    dgrad(1, both, 4, half)
    red_b.finish(3)
    red_b.start(4)
    red_c.finish(3)
    red_c.start(4)
    red_a.finish(4)
    red_a.start(6)
    red_a.finish(6)
    red_b.finish(4)
    red_c.finish(4)
    relay_done()
    pltpu.make_async_copy(dg_v, dg_v, out_sem.at[0]).wait()


def store_kernel(groups, sub, ups, dg_in, wg_in, dg_out, wg_out, half_v, wide_v, sem):
    dg_copy = pltpu.make_async_copy(dg_in, dg_out, sem.at[0])
    dg_copy.start()
    load = pltpu.make_async_copy(wg_in, half_v, sem.at[1])
    load.start()
    load.wait()
    outs = []

    def send(tap0, taps, slot):
        here = pl.ds(tap0 * ups, taps * ups)
        outs.append(pltpu.make_async_copy(wide_v.at[here], wg_out.at[here], sem.at[slot]))
        outs[-1].start()

    for i in range(2):
        for j in range(-(-9 * ups // sub)):
            n = min(sub, 9 * ups - j * sub)
            src = groups[0][0] + j * groups[0][1] + i * sub
            wide_v[pl.ds(9 * (i + 1) * ups + j * sub, n)] = half_v[pl.ds(src, n)].astype(jnp.float32)
    send(9, 18, 2)
    lanes = half_v.shape[2]
    left = lax.broadcasted_iota(jnp.int32, (ups * UNIT, lanes), 1) < lanes // 2

    def block(h, q):
        v = half_v[pl.ds(groups[1 + h][0] + q * ups, ups)].astype(jnp.float32)
        return v.reshape(ups * UNIT, lanes)

    def put(tap, low, high):
        wide_v[pl.ds(tap * ups, ups)] = jnp.where(left, low, high).reshape(ups, UNIT, lanes)

    def other(v):
        return pltpu.roll(v, lanes // 2, 1)

    for q, kh in enumerate((1, 2, 0)):
        put(kh * 3 + 2, block(0, q), other(block(1, q)))
        put(kh * 3, other(block(0, q)), block(1, q))
    put(4, block(0, 3), other(block(1, 3)))
    put(7, other(block(0, 3)), block(1, 3))
    put(1, block(0, 4), other(block(1, 4)))
    send(0, 9, 3)
    dg_copy.wait()
    for c in outs:
        c.wait()


def on_device(features, pre_act, cotangent, weight):
    c_in, planes_in, _, _, rows, cols = features.shape
    c_out, planes = pre_act.shape[:2]
    taps = weight.shape[0]
    chips = lax.axis_size("sp") // 2
    chs = lax.axis_size("ch")
    devices = chips * 2 * chs
    scale = 1.0 / math.sqrt(devices * planes * rows * cols)
    ups = c_in // UNIT
    sub = -(-9 * ups // (2 * chips))
    u_a = -(-2 * sub // chs) * chs
    u_b = -(-5 * ups // (2 * chips))
    span_b = u_b * 2 * chips
    groups = ((2 * span_b, u_a), (0, u_b), (span_b, u_b))
    units = u_a * 2 * chips + 2 * span_b
    parts = (2 * span_b, 2 * span_b + sub * 2 * chips)
    cfg = (chips, chs, rows, c_in, c_out, scale, groups, parts, sub)
    bf, f32 = jnp.bfloat16, jnp.float32
    span = rows * cols
    any_spec = pl.BlockSpec(memory_space=pl.ANY)

    def part(*lead, dtype=f32):
        return pltpu.VMEM(lead + (UNIT, c_out), dtype)

    held = 2 * units + (u_a + 2 * u_b) * (2 * chips + chs)
    vmem = 18 * 2**20 + held * UNIT * c_out * 4
    dg, wg = pl.pallas_call(
        functools.partial(kernel, cfg),
        out_shape=(
            jax.ShapeDtypeStruct((c_in, 2, 2, rows, 2, cols), bf),
            jax.ShapeDtypeStruct((units, UNIT, c_out), bf),
        ),
        in_specs=[pl.BlockSpec(memory_space=pltpu.HBM)] * 4,
        out_specs=(any_spec, any_spec),
        scratch_shapes=[
            pltpu.VMEM((rows, c_out, cols), bf),
            pltpu.VMEM((rows, c_out, cols), bf),
            pltpu.VMEM((2, 2, rows, c_in, 2, cols), bf),
            pltpu.VMEM(weight.shape, bf),
            pltpu.VMEM((rows, c_out, cols), bf),
            pltpu.VMEM((rows, c_out, cols), bf),
            pltpu.VMEM((2 * c_out, span + cols), bf),
            pltpu.VMEM((2 * c_out, span + cols), bf),
            pltpu.VMEM((2, 4 * c_in, span), bf),
            pltpu.VMEM((3, 6 * c_in, 2 * c_out), bf),
            pltpu.VMEM((2, 2 * c_in, c_out), f32),
            pltpu.VMEM((2, 6 * c_in, c_out), f32),
            pltpu.VMEM((2, 2, rows, c_in, 2, cols), bf),
            part(units),
            part(chs, u_a // chs, dtype=bf),
            part(u_b, dtype=bf),
            part(u_b, dtype=bf),
            part(sub * chips),
            part(sub * chips),
            part(chips - 1, sub),
            part(chips - 1, sub),
            part(2 * chips - 1, u_b),
            part(2 * chips - 1, u_b),
            part(chs, u_a // chs),
            part(chs - 1, u_a // chs),
            part(chs, u_b),
            part(chs, u_b),
            pltpu.VMEM((2 * rows, c_out // 2, cols), bf),
            pltpu.SemaphoreType.DMA((4,)),
            pltpu.SemaphoreType.DMA((4,)),
            pltpu.SemaphoreType.DMA((2,)),
            pltpu.SemaphoreType.DMA((2,)),
            pltpu.SemaphoreType.DMA((2,)),
            pltpu.SemaphoreType.DMA,
            pltpu.SemaphoreType.DMA((4, 6)),
            pltpu.SemaphoreType.DMA((4, 6)),
        ],
        compiler_params=pltpu.CompilerParams(
            collective_id=0, has_side_effects=True, vmem_limit_bytes=vmem
        ),
    )(
        pltpu.with_memory_space_constraint(pre_act.transpose(1, 2, 0, 3), pltpu.HBM),
        pltpu.with_memory_space_constraint(cotangent.transpose(1, 2, 0, 3), pltpu.HBM),
        pltpu.with_memory_space_constraint(features.transpose(0, 1, 2, 4, 3, 5), pltpu.HBM),
        pltpu.with_memory_space_constraint(weight, pltpu.HBM),
    )
    dg, wg = pl.pallas_call(
        functools.partial(store_kernel, groups, sub, ups),
        out_shape=(
            jax.ShapeDtypeStruct((c_in, planes_in, 2, rows, 2, cols), bf),
            jax.ShapeDtypeStruct((taps * ups, UNIT, c_out), f32),
        ),
        in_specs=[any_spec] * 2,
        out_specs=(pl.BlockSpec(memory_space=pltpu.HBM),) * 2,
        scratch_shapes=[
            part(units, dtype=bf),
            part(taps * ups),
            pltpu.SemaphoreType.DMA((4,)),
        ],
        compiler_params=pltpu.CompilerParams(vmem_limit_bytes=2**20 + (units + 2 * taps * ups) * UNIT * c_out * 2),
    )(dg, wg)
    return dg.transpose(0, 1, 2, 4, 3, 5), wg.reshape(taps, c_in, c_out)


def solution(mesh):
    return jax.shard_map(
        on_device,
        mesh=mesh,
        in_specs=(
            P(None, ("sp", "ch"), None, None, None, None),
            P(None, ("sp", "ch"), None, None),
            P(None, ("sp", "ch"), None, None),
            P(),
        ),
        out_specs=(P(None, ("sp", "ch"), None, None, None, None), P()),
        check_vma=False,
    )
```

```python
import functools
import math

import jax
import jax.numpy as jnp
from jax import lax
from jax.experimental import pallas as pl
from jax.experimental.pallas import tpu as pltpu
from jax.sharding import PartitionSpec as P

MESH = pl.DeviceIdType.MESH
LANES = 128
UNIT = 8


def kernel(cfg, pre_hbm, cot_hbm, feat_hbm, w_hbm, dg_out, wg_out, *scr):
    (pre_v, cot_v, feat_v, w_v, m_nat, h_nat, mh, mn, feat_a, wl, wf, ws, dg_v, grad, own_a, own_b, own_c) = scr[:17]
    (r1a, r1d, r2a, r2d, r2b, r2c, mid_a, r3a, r3b, r3c) = scr[17:27]
    relay_v, in_sem, out_sem, halo_s, halo_r, relay_s, relay_r, send_sem, recv_sem = scr[27:]
    chips, chs, rows, c_in, c_out, scale, groups, parts, sub = cfg
    sp = lax.axis_index("sp")
    ch = lax.axis_index("ch")
    chip = sp // 2
    core = sp % 2
    flat = sp * chs + ch
    last = chips * 2 * chs - 1
    span = rows * LANES

    def chip_dev(k, c):
        return (((chip + k) % chips) * 2 + c, ch)

    def ch_dev(k):
        return (sp, (ch + k) % chs)

    bar = pltpu.get_barrier_semaphore()
    prev = jnp.maximum(flat - 1, 0)
    nxt = jnp.minimum(flat + 1, last)

    @pl.when(flat > 0)
    def _():
        pl.semaphore_signal(bar, inc=1, device_id=(prev // chs, prev % chs), device_id_type=MESH)

    @pl.when(flat < last)
    def _():
        pl.semaphore_signal(bar, inc=1, device_id=(nxt // chs, nxt % chs), device_id_type=MESH)

    loads = [
        pltpu.make_async_copy(pre_hbm.at[0], pre_v, in_sem.at[0]),
        pltpu.make_async_copy(cot_hbm.at[0], cot_v, in_sem.at[1]),
        pltpu.make_async_copy(w_hbm, w_v, in_sem.at[2]),
    ]
    loads[0].start()
    loads[1].start()
    for k in range(1, chs):
        pl.semaphore_signal(bar, inc=1, device_id=ch_dev(k), device_id_type=MESH)
    for k in range(1, chips):
        pl.semaphore_signal(bar, inc=1, device_id=chip_dev(k, core), device_id_type=MESH)
    for k in range(chips):
        pl.semaphore_signal(bar, inc=1, device_id=chip_dev(k, 1 - core), device_id_type=MESH)
    loads[2].start()

    def load_feat(k, carry):
        p, s, b = k // (2 * rows), (k // rows) % 2, k % rows
        pltpu.make_async_copy(feat_hbm.at[:, p, s, b], feat_v.at[p, s, b], in_sem.at[3]).start()
        return carry

    lax.fori_loop(0, 4 * rows, load_feat, 0)

    loads[0].wait()
    loads[1].wait()

    def mask_step(b, carry):
        p = pre_v[b].astype(jnp.float32)
        m_nat[b] = jnp.where(p > 0, cot_v[b].astype(jnp.float32), 0.0).astype(jnp.bfloat16)
        return carry

    lax.fori_loop(0, rows, mask_step, 0)
    peers = 2 * chips + chs - 2 + jnp.minimum(flat, 1) + jnp.minimum(last - flat, 1)
    pl.semaphore_wait(bar, peers)

    hc = c_out // 2
    halos = [
        pltpu.make_async_remote_copy(
            src_ref=m_nat.at[:, pl.ds(h * hc, hc)], dst_ref=h_nat.at[:, pl.ds(h * hc, hc)],
            send_sem=halo_s.at[h], recv_sem=halo_r.at[h],
            device_id=(prev // chs, prev % chs), device_id_type=MESH,
        )
        for h in range(2)
    ]

    wrap = jnp.logical_and(core == 0, ch == 0) if chs > 1 else False

    @pl.when(jnp.logical_and(flat > 0, jnp.logical_not(wrap)))
    def _():
        halos[0].start()
        halos[1].start()

    def piece(h, lo, hi):
        return m_nat.at[pl.ds(lo, hi - lo), pl.ds(h * hc, hc)]

    def landing(h, lo, hi):
        return h_nat.at[pl.ds(lo, hi - lo), pl.ds(h * hc, hc)]

    def share(c):
        total = 3 * 2 * rows * (chips - c) // (chips * 4)
        return min(rows, total), max(0, total - rows)

    def send_wrap(c):
        ones, zeros = share(c)
        to, via = (2 * c - 1, chs - 1), (2 * c - 1, 0)
        for h, lo, hi, at in (
            (1, 0, ones, 0), (0, 0, zeros, ones), (0, zeros, rows, None), (1, ones, rows, None),
        ):
            if lo < hi:
                direct = at is None
                pltpu.make_async_remote_copy(
                    src_ref=piece(h, lo, hi),
                    dst_ref=landing(h, lo, hi) if direct else relay_v.at[pl.ds(at, hi - lo)],
                    send_sem=halo_s.at[h], recv_sem=halo_r.at[h] if direct else relay_r,
                    device_id=to if direct else via, device_id_type=MESH,
                ).start()

    for c in range(1, chips):
        if chs > 1:

            @pl.when(jnp.logical_and(wrap, chip == c))
            def _(c=c):
                send_wrap(c)

    def forwards(c):
        ones, zeros = share(c)
        return [
            pltpu.make_async_remote_copy(
                src_ref=relay_v.at[pl.ds(at, n)], dst_ref=landing(h, 0, n),
                send_sem=relay_s.at[h], recv_sem=halo_r.at[h],
                device_id=(sp, chs - 1), device_id_type=MESH,
            )
            for h, n, at in ((1, ones, 0), (0, zeros, ones))
            if n
        ]

    def at_relay(c):
        return jnp.logical_and(jnp.logical_and(core == 1, ch == 0), chip == c - 1)

    def relay():
        for c in range(1, chips if chs > 1 else 1):
            whole = relay_v.at[pl.ds(0, sum(share(c)))]

            @pl.when(at_relay(c))
            def _(c=c, whole=whole):
                pltpu.make_async_remote_copy(
                    src_ref=whole, dst_ref=whole, send_sem=relay_s.at[0], recv_sem=relay_r,
                    device_id=(sp, ch), device_id_type=MESH).wait_recv()
                for f in forwards(c):
                    f.start()

    def relay_done():
        for c in range(1, chips if chs > 1 else 1):

            @pl.when(at_relay(c))
            def _(c=c):
                for f in forwards(c):
                    f.wait_send()

    lane = lax.broadcasted_iota(jnp.int32, (c_out, LANES), 1)

    def spread(src, dst):
        dst[:, span:] = jnp.zeros((2 * c_out, LANES), jnp.bfloat16)
        for b in range(rows):
            v = src[b]
            dst[:c_out, b * LANES:(b + 1) * LANES] = v
            r = jnp.where(lane == LANES - 1, 0.0, pltpu.roll(v.astype(jnp.float32), LANES - 1, 1))
            dst[c_out:, b * LANES:(b + 1) * LANES] = r.astype(jnp.bfloat16)

    def spread_half(h):
        top, low = 2 * h * hc, (2 * h + 1) * hc
        mn[top:top + c_out, span:] = jnp.zeros((c_out, LANES), jnp.bfloat16)
        for b in range(rows):
            v = h_nat[b, h * hc:(h + 1) * hc]
            mn[top:low, b * LANES:(b + 1) * LANES] = v
            r = jnp.where(lane[:hc] == LANES - 1, 0.0, pltpu.roll(v.astype(jnp.float32), LANES - 1, 1))
            mn[low:low + hc, b * LANES:(b + 1) * LANES] = r.astype(jnp.bfloat16)

    spread(m_nat, mh)
    pltpu.make_async_copy(feat_v, feat_v, in_sem.at[3]).wait()
    two = 2 * c_in

    feat_rows = feat_v.reshape(2, 2, rows, two, LANES)

    def feat_step(k, carry):
        p, s = k // 2, k % 2
        at = pl.ds(pl.multiple_of(s * two, two), two)
        for b in range(rows):
            feat_a[p, at, b * LANES:(b + 1) * LANES] = feat_rows[p, s, b]
        return carry

    lax.fori_loop(0, 4, feat_step, 0)

    ups = c_in // UNIT
    starts = {1: parts[0], 2: parts[1]}

    def put(kd, kh, kw, val):
        base = starts[kd] + (kh * 3 + kw) * ups
        grad[base:base + ups] = val.reshape(ups, UNIT, c_out)

    def wgrad(kd, p, mm):
        dn = (((1,), (1,)), ((), ()))
        o = lax.dot_general(feat_a[p], mm[:, :span], dn, preferred_element_type=jnp.float32)
        d = lax.dot_general(feat_a[p, two:], mm[:, LANES:], dn, preferred_element_type=jnp.float32)
        for r in range(2):
            ws[r, :2 * two] = o[:, r * c_out:(r + 1) * c_out]
            ws[r, 2 * two:] = d[:, r * c_out:(r + 1) * c_out]
        for kh, part in ((1, 0), (2, 1), (0, 2)):
            for kw, r, t in ((1, 0, 0), (2, 0, 1), (0, 1, 1)):
                put(kd, kh, kw, ws[r, pl.ds(part * two + t, c_in, stride=2), :])

    left = lax.broadcasted_iota(jnp.int32, (c_in, c_out), 1) < hc

    def wgrad_half(h):
        dn = (((1,), (1,)), ((), ()))
        at = pl.ds(2 * h * hc, c_out)
        ws[0, :2 * two] = lax.dot_general(feat_a[1], mn[at, :span], dn, preferred_element_type=jnp.float32)
        ws[0, 2 * two:] = lax.dot_general(feat_a[1, two:], mn[at, LANES:], dn, preferred_element_type=jnp.float32)
        even = [ws[0, pl.ds(q * two, c_in, stride=2), :] for q in range(3)]
        odd = [ws[0, pl.ds(q * two + 1, c_in, stride=2), :] for q in range(3)]
        packed = jnp.where(left, even[0], pltpu.roll(even[1], hc, 1))
        for q, val in enumerate(odd + [packed, even[2]]):
            base = groups[1 + h][0] + q * ups
            grad[base:base + ups] = val.reshape(ups, UNIT, c_out)

    def weights():
        def step(kd, carry):
            for part, kh in enumerate((1, 2, 0)):
                base = kd * 9 + kh * 3
                wf[0, pl.ds(0, c_in, stride=2), :] = w_v[base + 1].astype(jnp.float32)
                wf[0, pl.ds(1, c_in, stride=2), :] = w_v[base + 2].astype(jnp.float32)
                wf[1, pl.ds(0, c_in, stride=2), :] = jnp.zeros((c_in, c_out), jnp.float32)
                wf[1, pl.ds(1, c_in, stride=2), :] = w_v[base].astype(jnp.float32)
                a, z = wf[0], wf[1]
                if swap:
                    a, z = jnp.where(wide, a, pltpu.roll(z, hc, 1)), jnp.where(wide, pltpu.roll(a, hc, 1), z)
                wl[kd, part * two:(part + 1) * two, :c_out] = a.astype(jnp.bfloat16)
                wl[kd, part * two:(part + 1) * two, c_out:] = z.astype(jnp.bfloat16)
            return carry

        wide = lax.broadcasted_iota(jnp.int32, (two, c_out), 1) < hc
        swap = True
        step(0, 0)
        swap = False
        lax.fori_loop(1, 3, step, 0)

    dg_rows = dg_v.reshape(2, 2, rows, two, LANES)

    def dgrad(p, terms, lo, hi):
        def step(k, carry):
            col = pl.multiple_of(k * 2 * LANES, 2 * LANES)
            here = pl.ds(col, 2 * LANES)
            down = pl.ds(pl.multiple_of(col + LANES, LANES), 2 * LANES)
            top, bot = None, None
            for kd, mm in terms:
                o = jnp.dot(wl[kd, :2 * two], mm[:, here], preferred_element_type=jnp.float32)
                d = jnp.dot(wl[kd, 2 * two:], mm[:, down], preferred_element_type=jnp.float32)
                top = o[:two] if top is None else top + o[:two]
                bot = o[two:] + d if bot is None else bot + (o[two:] + d)
            for s, val in ((0, top), (1, bot)):
                for j in range(2):
                    b = 2 * k + j
                    dg_rows[p, s, b] = val[:, j * LANES:(j + 1) * LANES].astype(jnp.bfloat16)
                    pltpu.make_async_copy(dg_v.at[p, s, b], dg_out.at[:, p, s, b], out_sem.at[0]).start()
            return carry

        lax.fori_loop(lo, hi, step, 0)

    class Early:
        def __init__(self, i, r1, r2):
            self.i, self.r1, self.r2 = i, r1, r2

        def off(self, a, k):
            return parts[self.i] + (a * chips + k) * sub

        def start(self, stage):
            cps = []
            if stage == 1:
                src = grad.at[pl.ds(self.off(1 - core, 0), sub * chips)]
                cps.append(self.remote(1, src, self.r1, chip_dev(0, 1 - core)))
            else:
                for k in range(1, chips):
                    src = grad.at[pl.ds(self.off(core, (chip + k) % chips), sub)]
                    cps.append(self.remote(2, src, self.r2.at[k - 1], chip_dev(k, core)))
            for c in cps:
                c.start()

        def remote(self, stage, src, dst, dev):
            at = (0, stage - 1 + 6 * self.i) if self.i == 0 else (3, stage - 1)
            return pltpu.make_async_remote_copy(
                src_ref=src, dst_ref=dst, send_sem=send_sem.at[at], recv_sem=recv_sem.at[at],
                device_id=dev, device_id_type=MESH)

        def finish(self, stage):
            buf = self.r1 if stage == 1 else self.r2
            whole = self.remote(stage, buf, buf, (sp, ch))
            whole.wait_send()
            whole.wait_recv()
            if stage == 1:
                s = pl.ds(self.off(core, 0), sub * chips)
                grad[s] = grad[s] + self.r1[...]
            else:
                v = grad[pl.ds(self.off(core, chip), sub)]
                for k in range(chips - 1):
                    v = v + self.r2[k]
                flat_mid = mid_a.reshape(groups[0][1], UNIT, c_out)
                flat_mid[self.i * sub:(self.i + 1) * sub] = v

    class Reduce:
        def __init__(self, idx, r1, r2, r3, own, mid=None):
            self.i, self.r1, self.r2, self.r3, self.own, self.mid = idx, r1, r2, r3, own, mid
            self.base, self.u = groups[idx]
            self.half = self.u * chips
            self.copies = {}

        def off(self, a, b):
            return self.base + a * self.half + b * self.u

        def remote(self, stage, src, dst, dev):
            return pltpu.make_async_remote_copy(
                src_ref=src, dst_ref=dst, send_sem=send_sem.at[self.i, stage - 1],
                recv_sem=recv_sem.at[self.i, stage - 1], device_id=dev, device_id_type=MESH)

        def start(self, stage):
            cps = []
            if stage == 1:
                src = grad.at[pl.ds(self.off(1 - core, 0), self.half)]
                cps.append(self.remote(1, src, self.r1, chip_dev(0, 1 - core)))
            elif stage == 2 and self.r1 is None:
                for j in range(1, 2 * chips):
                    k, c = j // 2, core if j % 2 == 0 else 1 - core
                    src = grad.at[pl.ds(self.off(c, (chip + k) % chips), self.u)]
                    cps.append(self.remote(2, src, self.r2.at[j - 1], chip_dev(k, c)))
            elif stage == 2:
                for k in range(1, chips):
                    src = grad.at[pl.ds(self.off(core, (chip + k) % chips), self.u)]
                    cps.append(self.remote(2, src, self.r2.at[k - 1], chip_dev(k, core)))
            elif stage == 3:
                for k in range(1, chs):
                    if self.mid is None:
                        src, dst = self.r3.at[ch], self.r3.at[ch]
                    else:
                        src, dst = self.mid.at[(ch + k) % chs], self.r3.at[k - 1]
                    cps.append(self.remote(3, src, dst, ch_dev(k)))
            elif stage == 6:
                ref = wg_out.at[pl.ds(self.off(core, 0), self.half)]
                cps.append(self.remote(6, ref, ref, chip_dev(0, 1 - core)))
            elif stage == 5:
                for k in range(1, chs):
                    cps.append(self.remote(5, self.own.at[ch], self.own.at[ch], ch_dev(k)))
            else:
                own, dst = self.own, wg_out.at[pl.ds(self.off(core, chip), self.u)]
                if self.mid is not None:
                    own = own.reshape(self.u, UNIT, c_out)
                for k in range(1, chips):
                    cps.append(self.remote(4, own, dst, chip_dev(k, core)))
                for k in range(chips if self.r1 is None else 0):
                    cps.append(self.remote(4, own, dst, chip_dev(k, 1 - core)))
                self.local = pltpu.make_async_copy(own, dst, out_sem.at[1 + self.i])
                self.local.start()
            for c in cps:
                c.start()
            self.copies[stage] = cps

        def finish(self, stage):
            if stage == 1:
                self.copies[1][0].wait()
                s = pl.ds(self.off(core, 0), self.half)
                grad[s] = grad[s] + self.r1[...]
            elif stage == 2:
                whole = pltpu.make_async_remote_copy(
                    src_ref=self.r2, dst_ref=self.r2, send_sem=send_sem.at[self.i, 1],
                    recv_sem=recv_sem.at[self.i, 1], device_id=(sp, ch), device_id_type=MESH)
                whole.wait_send()
                whole.wait_recv()
                v = grad[pl.ds(self.off(core, chip), self.u)]
                for k in range(self.r2.shape[0]):
                    v = v + self.r2[k]
                if self.mid is None:
                    self.r3[ch] = v
                else:
                    self.mid[...] = v.reshape(self.mid.shape)
            elif stage == 3:
                most = self.r3.at[pl.ds(0, chs - 1)]
                whole = pltpu.make_async_remote_copy(
                    src_ref=most, dst_ref=most, send_sem=send_sem.at[self.i, 2],
                    recv_sem=recv_sem.at[self.i, 2], device_id=(sp, ch), device_id_type=MESH)
                whole.wait_send()
                whole.wait_recv()
                if self.mid is None:
                    v = self.r3[0]
                    for k in range(1, chs):
                        v = v + self.r3[k]
                    self.own[...] = (v * scale).astype(self.own.dtype)
                else:
                    v = self.mid[ch]
                    for k in range(chs - 1):
                        v = v + self.r3[k]
                    self.own[ch] = (v * scale).astype(self.own.dtype)
            elif stage == 5:
                most = self.own.at[pl.ds(0, chs - 1)]
                whole = pltpu.make_async_remote_copy(
                    src_ref=most, dst_ref=most, send_sem=send_sem.at[self.i, 4],
                    recv_sem=recv_sem.at[self.i, 4], device_id=(sp, ch), device_id_type=MESH)
                whole.wait_send()
                whole.wait_recv()
            elif stage == 6:
                self.copies[6][0].wait()
            else:
                others = 2 * chips - 1 if self.r1 is None else chips - 1
                most = wg_out.at[pl.ds(self.base, others * self.u)]
                whole = pltpu.make_async_remote_copy(
                    src_ref=most, dst_ref=most, send_sem=send_sem.at[self.i, 3],
                    recv_sem=recv_sem.at[self.i, 3], device_id=(sp, ch), device_id_type=MESH)
                whole.wait_send()
                whole.wait_recv()
                self.local.wait()

    red_a = Reduce(0, r1a, None, r3a, own_a, mid_a)
    early = [Early(0, r1a, r2a), Early(1, r1d, r2d)]
    red_b = Reduce(1, None, r2b, r3b, own_b)
    red_c = Reduce(2, None, r2c, r3c, own_c)

    for lo, count, room in (
        (parts[0], 9 * ups, sub * 2 * chips),
        (parts[1], 9 * ups, sub * 2 * chips),
        (groups[1][0], 5 * ups, groups[1][1] * 2 * chips),
        (groups[2][0], 5 * ups, groups[2][1] * 2 * chips),
    ):
        if count < room:
            grad[lo + count:lo + room] = jnp.zeros((room - count, UNIT, LANES), jnp.float32)
    if 2 * sub < groups[0][1]:
        rest = mid_a.reshape(groups[0][1], UNIT, c_out)
        rest[2 * sub:] = jnp.zeros((groups[0][1] - 2 * sub, UNIT, LANES), jnp.float32)

    def halo_done(h):
        @pl.when(flat > 0)
        def _():
            halos[h].wait_send()

        @pl.when(flat < last)
        def _():
            halos[h].wait_recv()

        @pl.when(flat == last)
        def _():
            h_nat[:, h * hc:(h + 1) * hc] = jnp.zeros((rows, hc, LANES), jnp.bfloat16)

    half = rows // 2
    both = [(2, mh), (0, mn)]

    wgrad(1, 0, mh)
    early[0].start(1)
    wgrad(2, 1, mh)
    early[1].start(1)
    early[0].finish(1)
    early[0].start(2)
    loads[2].wait()
    weights()
    early[1].finish(1)
    early[1].start(2)
    dgrad(0, [(1, mh)], 0, 3)
    relay()
    dgrad(0, [(1, mh)], 3, half)
    early[0].finish(2)
    halo_done(0)
    spread_half(0)
    wgrad_half(0)
    red_b.start(2)

    early[1].finish(2)
    red_a.start(3)
    halo_done(1)
    spread_half(1)
    wgrad_half(1)
    red_c.start(2)
    red_a.finish(3)
    red_a.start(5)
    red_b.finish(2)
    red_b.start(3)
    dgrad(1, both, 0, 4)
    red_c.finish(2)
    red_c.start(3)
    red_a.finish(5)
    red_a.start(4)
    dgrad(1, both, 4, half)
    red_b.finish(3)
    red_b.start(4)
    red_c.finish(3)
    red_c.start(4)
    red_a.finish(4)
    red_a.start(6)
    red_a.finish(6)
    red_b.finish(4)
    red_c.finish(4)
    relay_done()
    pltpu.make_async_copy(dg_v, dg_v, out_sem.at[0]).wait()


def store_kernel(groups, sub, ups, dg_in, wg_in, dg_out, wg_out, half_v, wide_v, sem):
    dg_copy = pltpu.make_async_copy(dg_in, dg_out, sem.at[0])
    dg_copy.start()
    load = pltpu.make_async_copy(wg_in, half_v, sem.at[1])
    load.start()
    load.wait()
    outs = []

    def send(tap0, taps, slot):
        here = pl.ds(tap0 * ups, taps * ups)
        outs.append(pltpu.make_async_copy(wide_v.at[here], wg_out.at[here], sem.at[slot]))
        outs[-1].start()

    for i in range(2):
        for j in range(-(-9 * ups // sub)):
            n = min(sub, 9 * ups - j * sub)
            src = groups[0][0] + j * groups[0][1] + i * sub
            wide_v[pl.ds(9 * (i + 1) * ups + j * sub, n)] = half_v[pl.ds(src, n)].astype(jnp.float32)
    send(9, 18, 2)
    lanes = half_v.shape[2]
    left = lax.broadcasted_iota(jnp.int32, (ups * UNIT, lanes), 1) < lanes // 2

    def block(h, q):
        v = half_v[pl.ds(groups[1 + h][0] + q * ups, ups)].astype(jnp.float32)
        return v.reshape(ups * UNIT, lanes)

    def put(tap, low, high):
        wide_v[pl.ds(tap * ups, ups)] = jnp.where(left, low, high).reshape(ups, UNIT, lanes)

    def other(v):
        return pltpu.roll(v, lanes // 2, 1)

    for q, kh in enumerate((1, 2, 0)):
        put(kh * 3 + 2, block(0, q), other(block(1, q)))
        put(kh * 3, other(block(0, q)), block(1, q))
    put(4, block(0, 3), other(block(1, 3)))
    put(7, other(block(0, 3)), block(1, 3))
    put(1, block(0, 4), other(block(1, 4)))
    send(0, 9, 3)
    dg_copy.wait()
    for c in outs:
        c.wait()


def on_device(features, pre_act, cotangent, weight):
    c_in, planes_in, _, _, rows, cols = features.shape
    c_out, planes = pre_act.shape[:2]
    taps = weight.shape[0]
    chips = lax.axis_size("sp") // 2
    chs = lax.axis_size("ch")
    devices = chips * 2 * chs
    scale = 1.0 / math.sqrt(devices * planes * rows * cols)
    ups = c_in // UNIT
    sub = -(-9 * ups // (2 * chips))
    u_a = -(-2 * sub // chs) * chs
    u_b = -(-5 * ups // (2 * chips))
    span_b = u_b * 2 * chips
    groups = ((2 * span_b, u_a), (0, u_b), (span_b, u_b))
    units = u_a * 2 * chips + 2 * span_b
    parts = (2 * span_b, 2 * span_b + sub * 2 * chips)
    cfg = (chips, chs, rows, c_in, c_out, scale, groups, parts, sub)
    bf, f32 = jnp.bfloat16, jnp.float32
    span = rows * cols
    any_spec = pl.BlockSpec(memory_space=pl.ANY)

    def part(*lead, dtype=f32):
        return pltpu.VMEM(lead + (UNIT, c_out), dtype)

    held = 2 * units + (u_a + 2 * u_b) * (2 * chips + chs)
    vmem = 18 * 2**20 + held * UNIT * c_out * 4
    dg, wg = pl.pallas_call(
        functools.partial(kernel, cfg),
        out_shape=(
            jax.ShapeDtypeStruct((c_in, 2, 2, rows, 2, cols), bf),
            jax.ShapeDtypeStruct((units, UNIT, c_out), bf),
        ),
        in_specs=[pl.BlockSpec(memory_space=pltpu.HBM)] * 4,
        out_specs=(any_spec, any_spec),
        scratch_shapes=[
            pltpu.VMEM((rows, c_out, cols), bf),
            pltpu.VMEM((rows, c_out, cols), bf),
            pltpu.VMEM((2, 2, rows, c_in, 2, cols), bf),
            pltpu.VMEM(weight.shape, bf),
            pltpu.VMEM((rows, c_out, cols), bf),
            pltpu.VMEM((rows, c_out, cols), bf),
            pltpu.VMEM((2 * c_out, span + cols), bf),
            pltpu.VMEM((2 * c_out, span + cols), bf),
            pltpu.VMEM((2, 4 * c_in, span), bf),
            pltpu.VMEM((3, 6 * c_in, 2 * c_out), bf),
            pltpu.VMEM((2, 2 * c_in, c_out), f32),
            pltpu.VMEM((2, 6 * c_in, c_out), f32),
            pltpu.VMEM((2, 2, rows, c_in, 2, cols), bf),
            part(units),
            part(chs, u_a // chs, dtype=bf),
            part(u_b, dtype=bf),
            part(u_b, dtype=bf),
            part(sub * chips),
            part(sub * chips),
            part(chips - 1, sub),
            part(chips - 1, sub),
            part(2 * chips - 1, u_b),
            part(2 * chips - 1, u_b),
            part(chs, u_a // chs),
            part(chs - 1, u_a // chs),
            part(chs, u_b),
            part(chs, u_b),
            pltpu.VMEM((2 * rows, c_out // 2, cols), bf),
            pltpu.SemaphoreType.DMA((4,)),
            pltpu.SemaphoreType.DMA((4,)),
            pltpu.SemaphoreType.DMA((2,)),
            pltpu.SemaphoreType.DMA((2,)),
            pltpu.SemaphoreType.DMA((2,)),
            pltpu.SemaphoreType.DMA,
            pltpu.SemaphoreType.DMA((4, 6)),
            pltpu.SemaphoreType.DMA((4, 6)),
        ],
        compiler_params=pltpu.CompilerParams(
            collective_id=0, has_side_effects=True, vmem_limit_bytes=vmem
        ),
    )(
        pltpu.with_memory_space_constraint(pre_act.transpose(1, 2, 0, 3), pltpu.HBM),
        pltpu.with_memory_space_constraint(cotangent.transpose(1, 2, 0, 3), pltpu.HBM),
        pltpu.with_memory_space_constraint(features.transpose(0, 1, 2, 4, 3, 5), pltpu.HBM),
        pltpu.with_memory_space_constraint(weight, pltpu.HBM),
    )
    dg, wg = pl.pallas_call(
        functools.partial(store_kernel, groups, sub, ups),
        out_shape=(
            jax.ShapeDtypeStruct((c_in, planes_in, 2, rows, 2, cols), bf),
            jax.ShapeDtypeStruct((taps * ups, UNIT, c_out), f32),
        ),
        in_specs=[any_spec] * 2,
        out_specs=(pl.BlockSpec(memory_space=pltpu.HBM),) * 2,
        scratch_shapes=[
            part(units, dtype=bf),
            part(taps * ups),
            pltpu.SemaphoreType.DMA((4,)),
        ],
        compiler_params=pltpu.CompilerParams(vmem_limit_bytes=2**20 + (units + 2 * taps * ups) * UNIT * c_out * 2),
    )(dg, wg)
    return dg.transpose(0, 1, 2, 4, 3, 5), wg.reshape(taps, c_in, c_out)


def solution(mesh):
    return jax.shard_map(
        on_device,
        mesh=mesh,
        in_specs=(
            P(None, ("sp", "ch"), None, None, None, None),
            P(None, ("sp", "ch"), None, None),
            P(None, ("sp", "ch"), None, None),
            P(),
        ),
        out_specs=(P(None, ("sp", "ch"), None, None, None, None), P()),
        check_vma=False,
    )
```

```python
import functools
import math

import jax
import jax.numpy as jnp
from jax import lax
from jax.experimental import pallas as pl
from jax.experimental.pallas import tpu as pltpu
from jax.sharding import PartitionSpec as P

MESH = pl.DeviceIdType.MESH
LANES = 128
UNIT = 8


def kernel(cfg, pre_hbm, cot_hbm, feat_hbm, w_hbm, dg_out, wg_out, *scr):
    (pre_v, cot_v, feat_v, w_v, m_nat, h_nat, mh, mn, feat_a, wl, wf, ws, dg_v, grad, own_a, own_b, own_c) = scr[:17]
    (r1a, r1d, r2a, r2d, r2b, r2c, mid_a, r3a, r3b, r3c) = scr[17:27]
    relay_v, in_sem, out_sem, halo_s, halo_r, relay_s, relay_r, send_sem, recv_sem = scr[27:]
    chips, chs, rows, c_in, c_out, scale, groups, parts, sub = cfg
    sp = lax.axis_index("sp")
    ch = lax.axis_index("ch")
    chip = sp // 2
    core = sp % 2
    flat = sp * chs + ch
    last = chips * 2 * chs - 1
    span = rows * LANES

    def chip_dev(k, c):
        return (((chip + k) % chips) * 2 + c, ch)

    def ch_dev(k):
        return (sp, (ch + k) % chs)

    bar = pltpu.get_barrier_semaphore()
    prev = jnp.maximum(flat - 1, 0)
    nxt = jnp.minimum(flat + 1, last)

    @pl.when(flat > 0)
    def _():
        pl.semaphore_signal(bar, inc=1, device_id=(prev // chs, prev % chs), device_id_type=MESH)

    @pl.when(flat < last)
    def _():
        pl.semaphore_signal(bar, inc=1, device_id=(nxt // chs, nxt % chs), device_id_type=MESH)

    loads = [
        pltpu.make_async_copy(pre_hbm.at[0], pre_v, in_sem.at[0]),
        pltpu.make_async_copy(cot_hbm.at[0], cot_v, in_sem.at[1]),
        pltpu.make_async_copy(w_hbm, w_v, in_sem.at[2]),
    ]
    for k in range(1, chs):
        pl.semaphore_signal(bar, inc=1, device_id=ch_dev(k), device_id_type=MESH)
    for k in range(1, chips):
        pl.semaphore_signal(bar, inc=1, device_id=chip_dev(k, core), device_id_type=MESH)
    for k in range(chips):
        pl.semaphore_signal(bar, inc=1, device_id=chip_dev(k, 1 - core), device_id_type=MESH)
    loads[0].start()
    loads[1].start()
    loads[2].start()

    def load_feat(k, carry):
        p, s, b = k // (2 * rows), (k // rows) % 2, k % rows
        pltpu.make_async_copy(feat_hbm.at[:, p, s, b], feat_v.at[p, s, b], in_sem.at[3]).start()
        return carry

    lax.fori_loop(0, 4 * rows, load_feat, 0)

    loads[0].wait()
    loads[1].wait()

    def mask_step(b, carry):
        p = pre_v[b].astype(jnp.float32)
        m_nat[b] = jnp.where(p > 0, cot_v[b].astype(jnp.float32), 0.0).astype(jnp.bfloat16)
        return carry

    lax.fori_loop(0, rows, mask_step, 0, unroll=True)
    peers = 2 * chips + chs - 2 + jnp.minimum(flat, 1) + jnp.minimum(last - flat, 1)
    pl.semaphore_wait(bar, peers)

    hc = c_out // 2
    halos = [
        pltpu.make_async_remote_copy(
            src_ref=m_nat.at[:, pl.ds(h * hc, hc)], dst_ref=h_nat.at[:, pl.ds(h * hc, hc)],
            send_sem=halo_s.at[h], recv_sem=halo_r.at[h],
            device_id=(prev // chs, prev % chs), device_id_type=MESH,
        )
        for h in range(2)
    ]

    wrap = jnp.logical_and(core == 0, ch == 0) if chs > 1 else False

    @pl.when(jnp.logical_and(flat > 0, jnp.logical_not(wrap)))
    def _():
        halos[0].start()
        halos[1].start()

    def piece(h, lo, hi):
        return m_nat.at[pl.ds(lo, hi - lo), pl.ds(h * hc, hc)]

    def landing(h, lo, hi):
        return h_nat.at[pl.ds(lo, hi - lo), pl.ds(h * hc, hc)]

    def share(c):
        total = 7 * 2 * rows * (chips - c) // (8 * chips)
        return min(rows, total), max(0, total - rows)

    def legs(c, slot):
        ones, zeros = share(c)
        cut = (ones + zeros + 1) // 2
        lo, hi = (0, cut) if slot == 0 else (cut, ones + zeros)
        parts_of = ((1, lo, min(hi, ones), lo), (0, max(lo, ones) - ones, hi - ones, max(lo, ones)))
        return lo, hi, [p for p in parts_of if p[1] < p[2]]

    def send_wrap(c):
        ones, zeros = share(c)
        to, via = (2 * c - 1, chs - 1), (2 * c - 1, 0)
        for slot in range(2):
            for h, lo, hi, at in legs(c, slot)[2]:
                pltpu.make_async_remote_copy(
                    src_ref=piece(h, lo, hi), dst_ref=relay_v.at[pl.ds(at, hi - lo)],
                    send_sem=halo_s.at[h], recv_sem=relay_r.at[slot], device_id=via, device_id_type=MESH,
                ).start()
        for h, lo in ((0, zeros), (1, ones)):
            if lo < rows:
                pltpu.make_async_remote_copy(
                    src_ref=piece(h, lo, rows), dst_ref=landing(h, lo, rows),
                    send_sem=halo_s.at[h], recv_sem=halo_r.at[h], device_id=to, device_id_type=MESH,
                ).start()

    for c in range(1, chips):
        if chs > 1:

            @pl.when(jnp.logical_and(wrap, chip == c))
            def _(c=c):
                send_wrap(c)

    def forwards(c, slot):
        return [
            pltpu.make_async_remote_copy(
                src_ref=relay_v.at[pl.ds(at, hi - lo)], dst_ref=landing(h, lo, hi),
                send_sem=relay_s.at[slot], recv_sem=halo_r.at[h],
                device_id=(sp, chs - 1), device_id_type=MESH,
            )
            for h, lo, hi, at in legs(c, slot)[2]
        ]

    def at_relay(c):
        return jnp.logical_and(jnp.logical_and(core == 1, ch == 0), chip == c - 1)

    def relayed(c, slot):
        lo, hi, _ = legs(c, slot)
        whole = relay_v.at[pl.ds(lo, hi - lo)]
        return pltpu.make_async_remote_copy(
            src_ref=whole, dst_ref=whole, send_sem=relay_s.at[slot], recv_sem=relay_r.at[slot],
            device_id=(sp, ch), device_id_type=MESH)

    def relay(slot):
        for c in range(1, chips if chs > 1 else 1):
            if legs(c, slot)[2]:

                @pl.when(at_relay(c))
                def _(c=c):
                    relayed(c, slot).wait_recv()
                    for f in forwards(c, slot):
                        f.start()

    def relay_done():
        for c in range(1, chips if chs > 1 else 1):
            for slot in range(2):
                if legs(c, slot)[2]:

                    @pl.when(at_relay(c))
                    def _(c=c, slot=slot):
                        relayed(c, slot).wait_send()

    lane = lax.broadcasted_iota(jnp.int32, (c_out, LANES), 1)

    def spread(src, dst):
        dst[:, span:] = jnp.zeros((2 * c_out, LANES), jnp.bfloat16)
        for b in range(rows):
            v = src[b]
            dst[:c_out, b * LANES:(b + 1) * LANES] = v
            r = jnp.where(lane == LANES - 1, 0.0, pltpu.roll(v.astype(jnp.float32), LANES - 1, 1))
            dst[c_out:, b * LANES:(b + 1) * LANES] = r.astype(jnp.bfloat16)

    def spread_half(h):
        top, low = 2 * h * hc, (2 * h + 1) * hc
        mn[top:top + c_out, span:] = jnp.zeros((c_out, LANES), jnp.bfloat16)
        for b in range(rows):
            v = h_nat[b, h * hc:(h + 1) * hc]
            mn[top:low, b * LANES:(b + 1) * LANES] = v
            r = jnp.where(lane[:hc] == LANES - 1, 0.0, pltpu.roll(v.astype(jnp.float32), LANES - 1, 1))
            mn[low:low + hc, b * LANES:(b + 1) * LANES] = r.astype(jnp.bfloat16)

    spread(m_nat, mh)
    pltpu.make_async_copy(feat_v, feat_v, in_sem.at[3]).wait()
    two = 2 * c_in

    feat_rows = feat_v.reshape(2, 2, rows, two, LANES)

    def feat_step(k, carry):
        p, s = k // 2, k % 2
        at = pl.ds(pl.multiple_of(s * two, two), two)
        for b in range(rows):
            feat_a[p, at, b * LANES:(b + 1) * LANES] = feat_rows[p, s, b]
        return carry

    lax.fori_loop(0, 4, feat_step, 0)

    ups = c_in // UNIT
    starts = {1: parts[0], 2: parts[1]}

    def put(kd, kh, kw, val):
        base = starts[kd] + (kh * 3 + kw) * ups
        grad[base:base + ups] = val.reshape(ups, UNIT, c_out)

    def wgrad(kd, p, mm):
        dn = (((1,), (1,)), ((), ()))
        o = lax.dot_general(feat_a[p], mm[:, :span], dn, preferred_element_type=jnp.float32)
        d = lax.dot_general(feat_a[p, two:], mm[:, LANES:], dn, preferred_element_type=jnp.float32)
        for r in range(2):
            ws[r, :2 * two] = o[:, r * c_out:(r + 1) * c_out]
            ws[r, 2 * two:] = d[:, r * c_out:(r + 1) * c_out]
        for kh, part in ((1, 0), (2, 1), (0, 2)):
            for kw, r, t in ((1, 0, 0), (2, 0, 1), (0, 1, 1)):
                put(kd, kh, kw, ws[r, pl.ds(part * two + t, c_in, stride=2), :])

    left = lax.broadcasted_iota(jnp.int32, (c_in, c_out), 1) < hc

    def wgrad_half(h):
        dn = (((1,), (1,)), ((), ()))
        at = pl.ds(2 * h * hc, c_out)
        ws[0, :2 * two] = lax.dot_general(feat_a[1], mn[at, :span], dn, preferred_element_type=jnp.float32)
        ws[0, 2 * two:] = lax.dot_general(feat_a[1, two:], mn[at, LANES:], dn, preferred_element_type=jnp.float32)
        even = [ws[0, pl.ds(q * two, c_in, stride=2), :] for q in range(3)]
        odd = [ws[0, pl.ds(q * two + 1, c_in, stride=2), :] for q in range(3)]
        packed = jnp.where(left, even[0], pltpu.roll(even[1], hc, 1))
        for q, val in enumerate(odd + [packed, even[2]]):
            base = groups[1 + h][0] + q * ups
            grad[base:base + ups] = val.reshape(ups, UNIT, c_out)

    def weights():
        def step(kd, carry):
            for part, kh in enumerate((1, 2, 0)):
                base = kd * 9 + kh * 3
                wf[0, pl.ds(0, c_in, stride=2), :] = w_v[base + 1].astype(jnp.float32)
                wf[0, pl.ds(1, c_in, stride=2), :] = w_v[base + 2].astype(jnp.float32)
                wf[1, pl.ds(0, c_in, stride=2), :] = jnp.zeros((c_in, c_out), jnp.float32)
                wf[1, pl.ds(1, c_in, stride=2), :] = w_v[base].astype(jnp.float32)
                a, z = wf[0], wf[1]
                if swap:
                    a, z = jnp.where(wide, a, pltpu.roll(z, hc, 1)), jnp.where(wide, pltpu.roll(a, hc, 1), z)
                wl[kd, part * two:(part + 1) * two, :c_out] = a.astype(jnp.bfloat16)
                wl[kd, part * two:(part + 1) * two, c_out:] = z.astype(jnp.bfloat16)
            return carry

        wide = lax.broadcasted_iota(jnp.int32, (two, c_out), 1) < hc
        swap = True
        step(0, 0)
        swap = False
        lax.fori_loop(1, 3, step, 0)

    dg_rows = dg_v.reshape(2, 2, rows, two, LANES)

    def dgrad(p, terms, lo, hi):
        def step(k, carry):
            col = pl.multiple_of(k * 2 * LANES, 2 * LANES)
            here = pl.ds(col, 2 * LANES)
            down = pl.ds(pl.multiple_of(col + LANES, LANES), 2 * LANES)
            top, bot = None, None
            for kd, mm in terms:
                o = jnp.dot(wl[kd, :2 * two], mm[:, here], preferred_element_type=jnp.float32)
                d = jnp.dot(wl[kd, 2 * two:], mm[:, down], preferred_element_type=jnp.float32)
                top = o[:two] if top is None else top + o[:two]
                bot = o[two:] + d if bot is None else bot + (o[two:] + d)
            for s, val in ((0, top), (1, bot)):
                for j in range(2):
                    b = 2 * k + j
                    dg_rows[p, s, b] = val[:, j * LANES:(j + 1) * LANES].astype(jnp.bfloat16)
                    pltpu.make_async_copy(dg_v.at[p, s, b], dg_out.at[:, p, s, b], out_sem.at[0]).start()
            return carry

        lax.fori_loop(lo, hi, step, 0)

    sent = []

    class Early:
        def __init__(self, i, r1, r2):
            self.i, self.r1, self.r2 = i, r1, r2

        def off(self, a, k):
            return parts[self.i] + (a * chips + k) * sub

        def start(self, stage):
            cps = []
            if stage == 1:
                src = grad.at[pl.ds(self.off(1 - core, 0), sub * chips)]
                cps.append(self.remote(1, src, self.r1, chip_dev(0, 1 - core)))
            else:
                for k in range(1, chips):
                    src = grad.at[pl.ds(self.off(core, (chip + k) % chips), sub)]
                    cps.append(self.remote(2, src, self.r2.at[k - 1], chip_dev(k, core)))
            for c in cps:
                c.start()

        def remote(self, stage, src, dst, dev):
            at = (0, stage - 1 + 6 * self.i) if self.i == 0 else (3, stage - 1)
            return pltpu.make_async_remote_copy(
                src_ref=src, dst_ref=dst, send_sem=send_sem.at[at], recv_sem=recv_sem.at[at],
                device_id=dev, device_id_type=MESH)

        def finish(self, stage):
            buf = self.r1 if stage == 1 else self.r2
            whole = self.remote(stage, buf, buf, (sp, ch))
            whole.wait_recv()
            sent.append(whole)
            if stage == 1:
                s = pl.ds(self.off(core, 0), sub * chips)
                grad[s] = grad[s] + self.r1[...]
            else:
                v = grad[pl.ds(self.off(core, chip), sub)]
                for k in range(chips - 1):
                    v = v + self.r2[k]
                flat_mid = mid_a.reshape(groups[0][1], UNIT, c_out)
                flat_mid[self.i * sub:(self.i + 1) * sub] = v

    class Reduce:
        def __init__(self, idx, r1, r2, r3, own, mid=None):
            self.i, self.r1, self.r2, self.r3, self.own, self.mid = idx, r1, r2, r3, own, mid
            self.base, self.u = groups[idx]
            self.half = self.u * chips
            self.copies = {}

        def off(self, a, b):
            return self.base + a * self.half + b * self.u

        def remote(self, stage, src, dst, dev):
            return pltpu.make_async_remote_copy(
                src_ref=src, dst_ref=dst, send_sem=send_sem.at[self.i, stage - 1],
                recv_sem=recv_sem.at[self.i, stage - 1], device_id=dev, device_id_type=MESH)

        def start(self, stage):
            cps = []
            if stage == 1:
                src = grad.at[pl.ds(self.off(1 - core, 0), self.half)]
                cps.append(self.remote(1, src, self.r1, chip_dev(0, 1 - core)))
            elif stage == 2 and self.r1 is None:
                for j in range(1, 2 * chips):
                    k, c = j // 2, core if j % 2 == 0 else 1 - core
                    src = grad.at[pl.ds(self.off(c, (chip + k) % chips), self.u)]
                    cps.append(self.remote(2, src, self.r2.at[j - 1], chip_dev(k, c)))
            elif stage == 2:
                for k in range(1, chips):
                    src = grad.at[pl.ds(self.off(core, (chip + k) % chips), self.u)]
                    cps.append(self.remote(2, src, self.r2.at[k - 1], chip_dev(k, core)))
            elif stage == 3:
                for k in range(1, chs):
                    if self.mid is None:
                        src, dst = self.r3.at[ch], self.r3.at[ch]
                    else:
                        src, dst = self.mid.at[(ch + k) % chs], self.r3.at[k - 1]
                    cps.append(self.remote(3, src, dst, ch_dev(k)))
            elif stage == 6:
                ref = wg_out.at[pl.ds(self.off(core, 0), self.half)]
                cps.append(self.remote(6, ref, ref, chip_dev(0, 1 - core)))
            elif stage == 5:
                for k in range(1, chs):
                    cps.append(self.remote(5, self.own.at[ch], self.own.at[ch], ch_dev(k)))
            else:
                own, dst = self.own, wg_out.at[pl.ds(self.off(core, chip), self.u)]
                if self.mid is not None:
                    own = own.reshape(self.u, UNIT, c_out)
                for k in range(1, chips):
                    cps.append(self.remote(4, own, dst, chip_dev(k, core)))
                for k in range(chips if self.r1 is None else 0):
                    cps.append(self.remote(4, own, dst, chip_dev(k, 1 - core)))
                self.local = pltpu.make_async_copy(own, dst, out_sem.at[1 + self.i])
                self.local.start()
            for c in cps:
                c.start()
            self.copies[stage] = cps

        def finish(self, stage):
            if stage == 1:
                self.copies[1][0].wait_recv()
                sent.append(self.copies[1][0])
                s = pl.ds(self.off(core, 0), self.half)
                grad[s] = grad[s] + self.r1[...]
            elif stage == 2:
                whole = pltpu.make_async_remote_copy(
                    src_ref=self.r2, dst_ref=self.r2, send_sem=send_sem.at[self.i, 1],
                    recv_sem=recv_sem.at[self.i, 1], device_id=(sp, ch), device_id_type=MESH)
                whole.wait_recv()
                sent.append(whole)
                v = grad[pl.ds(self.off(core, chip), self.u)]
                for k in range(self.r2.shape[0]):
                    v = v + self.r2[k]
                if self.mid is None:
                    self.r3[ch] = v
                else:
                    self.mid[...] = v.reshape(self.mid.shape)
            elif stage == 3:
                most = self.r3.at[pl.ds(0, chs - 1)]
                whole = pltpu.make_async_remote_copy(
                    src_ref=most, dst_ref=most, send_sem=send_sem.at[self.i, 2],
                    recv_sem=recv_sem.at[self.i, 2], device_id=(sp, ch), device_id_type=MESH)
                whole.wait_recv()
                sent.append(whole)
                if self.mid is None:
                    v = self.r3[0]
                    for k in range(1, chs):
                        v = v + self.r3[k]
                    self.own[...] = (v * scale).astype(self.own.dtype)
                else:
                    v = self.mid[ch]
                    for k in range(chs - 1):
                        v = v + self.r3[k]
                    self.own[ch] = (v * scale).astype(self.own.dtype)
            elif stage == 5:
                most = self.own.at[pl.ds(0, chs - 1)]
                whole = pltpu.make_async_remote_copy(
                    src_ref=most, dst_ref=most, send_sem=send_sem.at[self.i, 4],
                    recv_sem=recv_sem.at[self.i, 4], device_id=(sp, ch), device_id_type=MESH)
                whole.wait_recv()
                sent.append(whole)
            elif stage == 6:
                self.copies[6][0].wait_recv()
                sent.append(self.copies[6][0])
            else:
                others = 2 * chips - 1 if self.r1 is None else chips - 1
                most = wg_out.at[pl.ds(self.base, others * self.u)]
                whole = pltpu.make_async_remote_copy(
                    src_ref=most, dst_ref=most, send_sem=send_sem.at[self.i, 3],
                    recv_sem=recv_sem.at[self.i, 3], device_id=(sp, ch), device_id_type=MESH)
                whole.wait_recv()
                sent.append(whole)
                self.local.wait()

    red_a = Reduce(0, r1a, None, r3a, own_a, mid_a)
    early = [Early(0, r1a, r2a), Early(1, r1d, r2d)]
    red_b = Reduce(1, None, r2b, r3b, own_b)
    red_c = Reduce(2, None, r2c, r3c, own_c)

    for lo, count, room in (
        (parts[0], 9 * ups, sub * 2 * chips),
        (parts[1], 9 * ups, sub * 2 * chips),
        (groups[1][0], 5 * ups, groups[1][1] * 2 * chips),
        (groups[2][0], 5 * ups, groups[2][1] * 2 * chips),
    ):
        if count < room:
            grad[lo + count:lo + room] = jnp.zeros((room - count, UNIT, LANES), jnp.float32)
    if 2 * sub < groups[0][1]:
        rest = mid_a.reshape(groups[0][1], UNIT, c_out)
        rest[2 * sub:] = jnp.zeros((groups[0][1] - 2 * sub, UNIT, LANES), jnp.float32)

    def all_sent():
        @pl.when(flat > 0)
        def _():
            halos[0].wait_send()
            halos[1].wait_send()

        for c in sent:
            c.wait_send()

    def halo_done(h):
        @pl.when(flat < last)
        def _():
            halos[h].wait_recv()

        @pl.when(flat == last)
        def _():
            h_nat[:, h * hc:(h + 1) * hc] = jnp.zeros((rows, hc, LANES), jnp.bfloat16)

    half = rows // 2
    both = [(2, mh), (0, mn)]

    wgrad(1, 0, mh)
    early[0].start(1)
    wgrad(2, 1, mh)
    early[1].start(1)
    early[0].finish(1)
    early[0].start(2)
    loads[2].wait()
    weights()
    early[1].finish(1)
    early[1].start(2)
    relay(0)
    dgrad(0, [(1, mh)], 0, 3)
    relay(1)
    dgrad(0, [(1, mh)], 3, half)
    early[0].finish(2)
    halo_done(0)
    spread_half(0)
    wgrad_half(0)
    red_b.start(2)

    early[1].finish(2)
    red_a.start(3)
    halo_done(1)
    spread_half(1)
    wgrad_half(1)
    red_c.start(2)
    red_a.finish(3)
    red_a.start(5)
    red_b.finish(2)
    red_b.start(3)
    dgrad(1, both, 0, 4)
    red_c.finish(2)
    red_c.start(3)
    red_a.finish(5)
    red_a.start(4)
    dgrad(1, both, 4, half)
    red_b.finish(3)
    red_b.start(4)
    red_c.finish(3)
    red_c.start(4)
    red_a.finish(4)
    red_a.start(6)
    red_a.finish(6)
    red_b.finish(4)
    red_c.finish(4)
    relay_done()
    all_sent()
    pltpu.make_async_copy(dg_v, dg_v, out_sem.at[0]).wait()


def store_kernel(groups, sub, ups, dg_in, wg_in, dg_out, wg_out, half_v, wide_v, sem):
    dg_copy = pltpu.make_async_copy(dg_in, dg_out, sem.at[0])
    dg_copy.start()
    load = pltpu.make_async_copy(wg_in, half_v, sem.at[1])
    load.start()
    load.wait()
    outs = []

    def send(tap0, taps, slot):
        here = pl.ds(tap0 * ups, taps * ups)
        outs.append(pltpu.make_async_copy(wide_v.at[here], wg_out.at[here], sem.at[slot]))
        outs[-1].start()

    for i in range(2):
        for j in range(-(-9 * ups // sub)):
            n = min(sub, 9 * ups - j * sub)
            src = groups[0][0] + j * groups[0][1] + i * sub
            wide_v[pl.ds(9 * (i + 1) * ups + j * sub, n)] = half_v[pl.ds(src, n)].astype(jnp.float32)
    send(9, 18, 2)
    lanes = half_v.shape[2]
    left = lax.broadcasted_iota(jnp.int32, (ups * UNIT, lanes), 1) < lanes // 2

    def block(h, q):
        v = half_v[pl.ds(groups[1 + h][0] + q * ups, ups)].astype(jnp.float32)
        return v.reshape(ups * UNIT, lanes)

    def put(tap, low, high):
        wide_v[pl.ds(tap * ups, ups)] = jnp.where(left, low, high).reshape(ups, UNIT, lanes)

    def other(v):
        return pltpu.roll(v, lanes // 2, 1)

    for q, kh in enumerate((1, 2, 0)):
        put(kh * 3 + 2, block(0, q), other(block(1, q)))
        put(kh * 3, other(block(0, q)), block(1, q))
    put(4, block(0, 3), other(block(1, 3)))
    put(7, other(block(0, 3)), block(1, 3))
    put(1, block(0, 4), other(block(1, 4)))
    send(0, 9, 3)
    dg_copy.wait()
    for c in outs:
        c.wait()


def on_device(features, pre_act, cotangent, weight):
    c_in, planes_in, _, _, rows, cols = features.shape
    c_out, planes = pre_act.shape[:2]
    taps = weight.shape[0]
    chips = lax.axis_size("sp") // 2
    chs = lax.axis_size("ch")
    devices = chips * 2 * chs
    scale = 1.0 / math.sqrt(devices * planes * rows * cols)
    ups = c_in // UNIT
    sub = -(-9 * ups // (2 * chips))
    u_a = -(-2 * sub // chs) * chs
    u_b = -(-5 * ups // (2 * chips))
    span_b = u_b * 2 * chips
    groups = ((2 * span_b, u_a), (0, u_b), (span_b, u_b))
    units = u_a * 2 * chips + 2 * span_b
    parts = (2 * span_b, 2 * span_b + sub * 2 * chips)
    cfg = (chips, chs, rows, c_in, c_out, scale, groups, parts, sub)
    bf, f32 = jnp.bfloat16, jnp.float32
    span = rows * cols
    any_spec = pl.BlockSpec(memory_space=pl.ANY)

    def part(*lead, dtype=f32):
        return pltpu.VMEM(lead + (UNIT, c_out), dtype)

    held = 2 * units + (u_a + 2 * u_b) * (2 * chips + chs)
    vmem = 18 * 2**20 + held * UNIT * c_out * 4
    dg, wg = pl.pallas_call(
        functools.partial(kernel, cfg),
        out_shape=(
            jax.ShapeDtypeStruct((c_in, 2, 2, rows, 2, cols), bf),
            jax.ShapeDtypeStruct((units, UNIT, c_out), bf),
        ),
        in_specs=[pl.BlockSpec(memory_space=pltpu.HBM)] * 4,
        out_specs=(any_spec, any_spec),
        scratch_shapes=[
            pltpu.VMEM((rows, c_out, cols), bf),
            pltpu.VMEM((rows, c_out, cols), bf),
            pltpu.VMEM((2, 2, rows, c_in, 2, cols), bf),
            pltpu.VMEM(weight.shape, bf),
            pltpu.VMEM((rows, c_out, cols), bf),
            pltpu.VMEM((rows, c_out, cols), bf),
            pltpu.VMEM((2 * c_out, span + cols), bf),
            pltpu.VMEM((2 * c_out, span + cols), bf),
            pltpu.VMEM((2, 4 * c_in, span), bf),
            pltpu.VMEM((3, 6 * c_in, 2 * c_out), bf),
            pltpu.VMEM((2, 2 * c_in, c_out), f32),
            pltpu.VMEM((2, 6 * c_in, c_out), f32),
            pltpu.VMEM((2, 2, rows, c_in, 2, cols), bf),
            part(units),
            part(chs, u_a // chs, dtype=bf),
            part(u_b, dtype=bf),
            part(u_b, dtype=bf),
            part(sub * chips),
            part(sub * chips),
            part(chips - 1, sub),
            part(chips - 1, sub),
            part(2 * chips - 1, u_b),
            part(2 * chips - 1, u_b),
            part(chs, u_a // chs),
            part(chs - 1, u_a // chs),
            part(chs, u_b),
            part(chs, u_b),
            pltpu.VMEM((2 * rows, c_out // 2, cols), bf),
            pltpu.SemaphoreType.DMA((4,)),
            pltpu.SemaphoreType.DMA((4,)),
            pltpu.SemaphoreType.DMA((2,)),
            pltpu.SemaphoreType.DMA((2,)),
            pltpu.SemaphoreType.DMA((2,)),
            pltpu.SemaphoreType.DMA((2,)),
            pltpu.SemaphoreType.DMA((4, 6)),
            pltpu.SemaphoreType.DMA((4, 6)),
        ],
        compiler_params=pltpu.CompilerParams(
            collective_id=0, has_side_effects=True, vmem_limit_bytes=vmem
        ),
    )(
        pltpu.with_memory_space_constraint(pre_act.transpose(1, 2, 0, 3), pltpu.HBM),
        pltpu.with_memory_space_constraint(cotangent.transpose(1, 2, 0, 3), pltpu.HBM),
        pltpu.with_memory_space_constraint(features.transpose(0, 1, 2, 4, 3, 5), pltpu.HBM),
        pltpu.with_memory_space_constraint(weight, pltpu.HBM),
    )
    dg, wg = pl.pallas_call(
        functools.partial(store_kernel, groups, sub, ups),
        out_shape=(
            jax.ShapeDtypeStruct((c_in, planes_in, 2, rows, 2, cols), bf),
            jax.ShapeDtypeStruct((taps * ups, UNIT, c_out), f32),
        ),
        in_specs=[any_spec] * 2,
        out_specs=(pl.BlockSpec(memory_space=pltpu.HBM),) * 2,
        scratch_shapes=[
            part(units, dtype=bf),
            part(taps * ups),
            pltpu.SemaphoreType.DMA((4,)),
        ],
        compiler_params=pltpu.CompilerParams(vmem_limit_bytes=2**20 + (units + 2 * taps * ups) * UNIT * c_out * 2),
    )(dg, wg)
    return dg.transpose(0, 1, 2, 4, 3, 5), wg.reshape(taps, c_in, c_out)


def solution(mesh):
    return jax.shard_map(
        on_device,
        mesh=mesh,
        in_specs=(
            P(None, ("sp", "ch"), None, None, None, None),
            P(None, ("sp", "ch"), None, None),
            P(None, ("sp", "ch"), None, None),
            P(),
        ),
        out_specs=(P(None, ("sp", "ch"), None, None, None, None), P()),
        check_vma=False,
    )
```

```python
import functools
import math

import jax
import jax.numpy as jnp
from jax import lax
from jax.experimental import pallas as pl
from jax.experimental.pallas import tpu as pltpu
from jax.sharding import PartitionSpec as P

MESH = pl.DeviceIdType.MESH
LANES = 128
UNIT = 8


def kernel(cfg, pre_hbm, cot_hbm, feat_hbm, w_hbm, dg_out, wg_out, *scr):
    (pre_v, cot_v, feat_v, w_v, m_nat, h_nat, mh, mn, feat_a, wl, wf, ws, dg_v, grad, own_a, own_b, own_c) = scr[:17]
    (r1a, r1d, r2a, r2d, r2b, r2c, mid_a, r3a, r3b, r3c) = scr[17:27]
    relay_v, in_sem, out_sem, halo_s, halo_r, relay_s, relay_r, send_sem, recv_sem = scr[27:]
    chips, chs, rows, c_in, c_out, scale, groups, parts, sub = cfg
    sp = lax.axis_index("sp")
    ch = lax.axis_index("ch")
    chip = sp // 2
    core = sp % 2
    flat = sp * chs + ch
    last = chips * 2 * chs - 1
    span = rows * LANES

    def chip_dev(k, c):
        return (((chip + k) % chips) * 2 + c, ch)

    def ch_dev(k):
        return (sp, (ch + k) % chs)

    bar = pltpu.get_barrier_semaphore()
    prev = jnp.maximum(flat - 1, 0)
    nxt = jnp.minimum(flat + 1, last)

    @pl.when(flat > 0)
    def _():
        pl.semaphore_signal(bar, inc=1, device_id=(prev // chs, prev % chs), device_id_type=MESH)

    @pl.when(flat < last)
    def _():
        pl.semaphore_signal(bar, inc=1, device_id=(nxt // chs, nxt % chs), device_id_type=MESH)

    loads = [
        pltpu.make_async_copy(pre_hbm.at[0], pre_v, in_sem.at[0]),
        pltpu.make_async_copy(cot_hbm.at[0], cot_v, in_sem.at[1]),
        pltpu.make_async_copy(w_hbm, w_v, in_sem.at[2]),
    ]
    for k in range(1, chs):
        pl.semaphore_signal(bar, inc=1, device_id=ch_dev(k), device_id_type=MESH)
    for k in range(1, chips):
        pl.semaphore_signal(bar, inc=1, device_id=chip_dev(k, core), device_id_type=MESH)
    for k in range(chips):
        pl.semaphore_signal(bar, inc=1, device_id=chip_dev(k, 1 - core), device_id_type=MESH)
    loads[0].start()
    loads[1].start()
    loads[2].start()

    def load_feat(k, carry):
        p, s, b = k // (2 * rows), (k // rows) % 2, k % rows
        pltpu.make_async_copy(feat_hbm.at[:, p, s, b], feat_v.at[p, s, b], in_sem.at[3]).start()
        return carry

    lax.fori_loop(0, 4 * rows, load_feat, 0)

    loads[0].wait()
    loads[1].wait()

    def mask_step(b, carry):
        p = pre_v[b].astype(jnp.float32)
        m_nat[b] = jnp.where(p > 0, cot_v[b].astype(jnp.float32), 0.0).astype(jnp.bfloat16)
        return carry

    lax.fori_loop(0, rows, mask_step, 0, unroll=True)
    peers = 2 * chips + chs - 2 + jnp.minimum(flat, 1) + jnp.minimum(last - flat, 1)
    pl.semaphore_wait(bar, peers)

    hc = c_out // 2
    halos = [
        pltpu.make_async_remote_copy(
            src_ref=m_nat.at[:, pl.ds(h * hc, hc)], dst_ref=h_nat.at[:, pl.ds(h * hc, hc)],
            send_sem=halo_s.at[h], recv_sem=halo_r.at[h],
            device_id=(prev // chs, prev % chs), device_id_type=MESH,
        )
        for h in range(2)
    ]

    wrap = jnp.logical_and(core == 0, ch == 0) if chs > 1 else False

    @pl.when(jnp.logical_and(flat > 0, jnp.logical_not(wrap)))
    def _():
        halos[0].start()
        halos[1].start()

    def piece(h, lo, hi):
        return m_nat.at[pl.ds(lo, hi - lo), pl.ds(h * hc, hc)]

    def landing(h, lo, hi):
        return h_nat.at[pl.ds(lo, hi - lo), pl.ds(h * hc, hc)]

    def share(c):
        total = 7 * 2 * rows * (chips - c) // (8 * chips)
        return min(rows, total), max(0, total - rows)

    def legs(c, slot):
        ones, zeros = share(c)
        cut = (ones + zeros + 1) // 2
        lo, hi = (0, cut) if slot == 0 else (cut, ones + zeros)
        parts_of = ((1, lo, min(hi, ones), lo), (0, max(lo, ones) - ones, hi - ones, max(lo, ones)))
        return lo, hi, [p for p in parts_of if p[1] < p[2]]

    def send_wrap(c):
        ones, zeros = share(c)
        to, via = (2 * c - 1, chs - 1), (2 * c - 1, 0)
        for slot in range(2):
            for h, lo, hi, at in legs(c, slot)[2]:
                pltpu.make_async_remote_copy(
                    src_ref=piece(h, lo, hi), dst_ref=relay_v.at[pl.ds(at, hi - lo)],
                    send_sem=halo_s.at[h], recv_sem=relay_r.at[slot], device_id=via, device_id_type=MESH,
                ).start()
        for h, lo in ((0, zeros), (1, ones)):
            if lo < rows:
                pltpu.make_async_remote_copy(
                    src_ref=piece(h, lo, rows), dst_ref=landing(h, lo, rows),
                    send_sem=halo_s.at[h], recv_sem=halo_r.at[h], device_id=to, device_id_type=MESH,
                ).start()

    for c in range(1, chips):
        if chs > 1:

            @pl.when(jnp.logical_and(wrap, chip == c))
            def _(c=c):
                send_wrap(c)

    def forwards(c, slot):
        return [
            pltpu.make_async_remote_copy(
                src_ref=relay_v.at[pl.ds(at, hi - lo)], dst_ref=landing(h, lo, hi),
                send_sem=relay_s.at[slot], recv_sem=halo_r.at[h],
                device_id=(sp, chs - 1), device_id_type=MESH,
            )
            for h, lo, hi, at in legs(c, slot)[2]
        ]

    def at_relay(c):
        return jnp.logical_and(jnp.logical_and(core == 1, ch == 0), chip == c - 1)

    def relayed(c, slot):
        lo, hi, _ = legs(c, slot)
        whole = relay_v.at[pl.ds(lo, hi - lo)]
        return pltpu.make_async_remote_copy(
            src_ref=whole, dst_ref=whole, send_sem=relay_s.at[slot], recv_sem=relay_r.at[slot],
            device_id=(sp, ch), device_id_type=MESH)

    def relay(slot):
        for c in range(1, chips if chs > 1 else 1):
            if legs(c, slot)[2]:

                @pl.when(at_relay(c))
                def _(c=c):
                    relayed(c, slot).wait_recv()
                    for f in forwards(c, slot):
                        f.start()

    def relay_done():
        for c in range(1, chips if chs > 1 else 1):
            for slot in range(2):
                if legs(c, slot)[2]:

                    @pl.when(at_relay(c))
                    def _(c=c, slot=slot):
                        relayed(c, slot).wait_send()

    lane = lax.broadcasted_iota(jnp.int32, (c_out, LANES), 1)

    def spread(src, dst):
        dst[:, span:] = jnp.zeros((2 * c_out, LANES), jnp.bfloat16)
        for b in range(rows):
            v = src[b]
            dst[:c_out, b * LANES:(b + 1) * LANES] = v
            r = jnp.where(lane == LANES - 1, 0.0, pltpu.roll(v.astype(jnp.float32), LANES - 1, 1))
            dst[c_out:, b * LANES:(b + 1) * LANES] = r.astype(jnp.bfloat16)

    def spread_half(h):
        top, low = 2 * h * hc, (2 * h + 1) * hc
        mn[top:top + c_out, span:] = jnp.zeros((c_out, LANES), jnp.bfloat16)
        for b in range(rows):
            v = h_nat[b, h * hc:(h + 1) * hc]
            mn[top:low, b * LANES:(b + 1) * LANES] = v
            r = jnp.where(lane[:hc] == LANES - 1, 0.0, pltpu.roll(v.astype(jnp.float32), LANES - 1, 1))
            mn[low:low + hc, b * LANES:(b + 1) * LANES] = r.astype(jnp.bfloat16)

    spread(m_nat, mh)
    pltpu.make_async_copy(feat_v, feat_v, in_sem.at[3]).wait()
    two = 2 * c_in

    feat_rows = feat_v.reshape(2, 2, rows, two, LANES)

    def feat_step(k, carry):
        p, s = k // 2, k % 2
        at = pl.ds(pl.multiple_of(s * two, two), two)
        for b in range(rows):
            feat_a[p, at, b * LANES:(b + 1) * LANES] = feat_rows[p, s, b]
        return carry

    lax.fori_loop(0, 4, feat_step, 0)

    ups = c_in // UNIT
    starts = {1: parts[0], 2: parts[1]}

    def put(kd, kh, kw, val):
        base = starts[kd] + (kh * 3 + kw) * ups
        grad[base:base + ups] = val.reshape(ups, UNIT, c_out)

    def wgrad(kd, p, mm):
        dn = (((1,), (1,)), ((), ()))
        o = lax.dot_general(feat_a[p], mm[:, :span], dn, preferred_element_type=jnp.float32)
        d = lax.dot_general(feat_a[p, two:], mm[:, LANES:], dn, preferred_element_type=jnp.float32)
        for r in range(2):
            ws[r, :2 * two] = o[:, r * c_out:(r + 1) * c_out]
            ws[r, 2 * two:] = d[:, r * c_out:(r + 1) * c_out]
        for kh, part in ((1, 0), (2, 1), (0, 2)):
            for kw, r, t in ((1, 0, 0), (2, 0, 1), (0, 1, 1)):
                put(kd, kh, kw, ws[r, pl.ds(part * two + t, c_in, stride=2), :])

    left = lax.broadcasted_iota(jnp.int32, (c_in, c_out), 1) < hc

    def wgrad_half(h):
        dn = (((1,), (1,)), ((), ()))
        at = pl.ds(2 * h * hc, c_out)
        ws[0, :2 * two] = lax.dot_general(feat_a[1], mn[at, :span], dn, preferred_element_type=jnp.float32)
        ws[0, 2 * two:] = lax.dot_general(feat_a[1, two:], mn[at, LANES:], dn, preferred_element_type=jnp.float32)
        even = [ws[0, pl.ds(q * two, c_in, stride=2), :] for q in range(3)]
        odd = [ws[0, pl.ds(q * two + 1, c_in, stride=2), :] for q in range(3)]
        packed = jnp.where(left, even[0], pltpu.roll(even[1], hc, 1))
        for q, val in enumerate(odd + [packed, even[2]]):
            base = groups[1 + h][0] + q * ups
            grad[base:base + ups] = val.reshape(ups, UNIT, c_out)

    def weights():
        def step(kd, carry):
            for part, kh in enumerate((1, 2, 0)):
                base = kd * 9 + kh * 3
                wf[0, pl.ds(0, c_in, stride=2), :] = w_v[base + 1].astype(jnp.float32)
                wf[0, pl.ds(1, c_in, stride=2), :] = w_v[base + 2].astype(jnp.float32)
                wf[1, pl.ds(0, c_in, stride=2), :] = jnp.zeros((c_in, c_out), jnp.float32)
                wf[1, pl.ds(1, c_in, stride=2), :] = w_v[base].astype(jnp.float32)
                a, z = wf[0], wf[1]
                if swap:
                    a, z = jnp.where(wide, a, pltpu.roll(z, hc, 1)), jnp.where(wide, pltpu.roll(a, hc, 1), z)
                wl[kd, part * two:(part + 1) * two, :c_out] = a.astype(jnp.bfloat16)
                wl[kd, part * two:(part + 1) * two, c_out:] = z.astype(jnp.bfloat16)
            return carry

        wide = lax.broadcasted_iota(jnp.int32, (two, c_out), 1) < hc
        swap = True
        step(0, 0)
        swap = False
        lax.fori_loop(1, 3, step, 0)

    dg_rows = dg_v.reshape(2, 2, rows, two, LANES)

    def dgrad(p, terms, lo, hi):
        def step(k, carry):
            col = pl.multiple_of(k * 2 * LANES, 2 * LANES)
            here = pl.ds(col, 2 * LANES)
            down = pl.ds(pl.multiple_of(col + LANES, LANES), 2 * LANES)
            top, bot = None, None
            for kd, mm in terms:
                o = jnp.dot(wl[kd, :2 * two], mm[:, here], preferred_element_type=jnp.float32)
                d = jnp.dot(wl[kd, 2 * two:], mm[:, down], preferred_element_type=jnp.float32)
                top = o[:two] if top is None else top + o[:two]
                bot = o[two:] + d if bot is None else bot + (o[two:] + d)
            for s, val in ((0, top), (1, bot)):
                for j in range(2):
                    b = 2 * k + j
                    dg_rows[p, s, b] = val[:, j * LANES:(j + 1) * LANES].astype(jnp.bfloat16)
                    pltpu.make_async_copy(dg_v.at[p, s, b], dg_out.at[:, p, s, b], out_sem.at[0]).start()
            return carry

        lax.fori_loop(lo, hi, step, 0)

    def slot(i, k):
        return k + {0: 0, 3: 6, 1: 7, 2: 10}[i]

    sent = []

    class Early:
        def __init__(self, i, r1, r2):
            self.i, self.r1, self.r2 = i, r1, r2

        def off(self, a, k):
            return parts[self.i] + (a * chips + k) * sub

        def start(self, stage):
            cps = []
            if stage == 1:
                src = grad.at[pl.ds(self.off(1 - core, 0), sub * chips)]
                cps.append(self.remote(1, src, self.r1, chip_dev(0, 1 - core)))
            else:
                for k in range(1, chips):
                    src = grad.at[pl.ds(self.off(core, (chip + k) % chips), sub)]
                    cps.append(self.remote(2, src, self.r2.at[k - 1], chip_dev(k, core)))
            for c in cps:
                c.start()

        def remote(self, stage, src, dst, dev):
            at = slot(0 if self.i == 0 else 3, stage - 1)
            return pltpu.make_async_remote_copy(
                src_ref=src, dst_ref=dst, send_sem=send_sem.at[at], recv_sem=recv_sem.at[at],
                device_id=dev, device_id_type=MESH)

        def finish(self, stage):
            buf = self.r1 if stage == 1 else self.r2
            whole = self.remote(stage, buf, buf, (sp, ch))
            whole.wait_recv()
            sent.append(whole)
            if stage == 1:
                s = pl.ds(self.off(core, 0), sub * chips)
                grad[s] = grad[s] + self.r1[...]
            else:
                v = grad[pl.ds(self.off(core, chip), sub)]
                for k in range(chips - 1):
                    v = v + self.r2[k]
                flat_mid = mid_a.reshape(groups[0][1], UNIT, c_out)
                flat_mid[self.i * sub:(self.i + 1) * sub] = v

    class Reduce:
        def __init__(self, idx, r1, r2, r3, own, mid=None):
            self.i, self.r1, self.r2, self.r3, self.own, self.mid = idx, r1, r2, r3, own, mid
            self.base, self.u = groups[idx]
            self.half = self.u * chips
            self.copies = {}

        def off(self, a, b):
            return self.base + a * self.half + b * self.u

        def remote(self, stage, src, dst, dev):
            return pltpu.make_async_remote_copy(
                src_ref=src, dst_ref=dst, send_sem=send_sem.at[slot(self.i, stage - 1)],
                recv_sem=recv_sem.at[slot(self.i, stage - 1)], device_id=dev, device_id_type=MESH)

        def start(self, stage):
            cps = []
            if stage == 1:
                src = grad.at[pl.ds(self.off(1 - core, 0), self.half)]
                cps.append(self.remote(1, src, self.r1, chip_dev(0, 1 - core)))
            elif stage == 2 and self.r1 is None:
                for j in range(1, 2 * chips):
                    k, c = j // 2, core if j % 2 == 0 else 1 - core
                    src = grad.at[pl.ds(self.off(c, (chip + k) % chips), self.u)]
                    cps.append(self.remote(2, src, self.r2.at[j - 1], chip_dev(k, c)))
            elif stage == 2:
                for k in range(1, chips):
                    src = grad.at[pl.ds(self.off(core, (chip + k) % chips), self.u)]
                    cps.append(self.remote(2, src, self.r2.at[k - 1], chip_dev(k, core)))
            elif stage == 3:
                for k in range(1, chs):
                    if self.mid is None:
                        src, dst = self.r3.at[ch], self.r3.at[ch]
                    else:
                        src, dst = self.mid.at[(ch + k) % chs], self.r3.at[k - 1]
                    cps.append(self.remote(3, src, dst, ch_dev(k)))
            elif stage == 6:
                ref = wg_out.at[pl.ds(self.off(core, 0), self.half)]
                cps.append(self.remote(6, ref, ref, chip_dev(0, 1 - core)))
            elif stage == 5:
                for k in range(1, chs):
                    cps.append(self.remote(5, self.own.at[ch], self.own.at[ch], ch_dev(k)))
            else:
                own, dst = self.own, wg_out.at[pl.ds(self.off(core, chip), self.u)]
                if self.mid is not None:
                    own = own.reshape(self.u, UNIT, c_out)
                for k in range(1, chips):
                    cps.append(self.remote(4, own, dst, chip_dev(k, core)))
                for k in range(chips if self.r1 is None else 0):
                    cps.append(self.remote(4, own, dst, chip_dev(k, 1 - core)))
                self.local = pltpu.make_async_copy(own, dst, out_sem.at[1 + self.i])
                self.local.start()
            for c in cps:
                c.start()
            self.copies[stage] = cps

        def finish(self, stage):
            if stage == 1:
                self.copies[1][0].wait_recv()
                sent.append(self.copies[1][0])
                s = pl.ds(self.off(core, 0), self.half)
                grad[s] = grad[s] + self.r1[...]
            elif stage == 2:
                whole = pltpu.make_async_remote_copy(
                    src_ref=self.r2, dst_ref=self.r2, send_sem=send_sem.at[slot(self.i, 1)],
                    recv_sem=recv_sem.at[slot(self.i, 1)], device_id=(sp, ch), device_id_type=MESH)
                whole.wait_recv()
                sent.append(whole)
                v = grad[pl.ds(self.off(core, chip), self.u)]
                for k in range(self.r2.shape[0]):
                    v = v + self.r2[k]
                if self.mid is None:
                    self.r3[ch] = v
                else:
                    self.mid[...] = v.reshape(self.mid.shape)
            elif stage == 3:
                most = self.r3.at[pl.ds(0, chs - 1)]
                whole = pltpu.make_async_remote_copy(
                    src_ref=most, dst_ref=most, send_sem=send_sem.at[slot(self.i, 2)],
                    recv_sem=recv_sem.at[slot(self.i, 2)], device_id=(sp, ch), device_id_type=MESH)
                whole.wait_recv()
                sent.append(whole)
                if self.mid is None:
                    v = self.r3[0]
                    for k in range(1, chs):
                        v = v + self.r3[k]
                    self.own[...] = (v * scale).astype(self.own.dtype)
                else:
                    v = self.mid[ch]
                    for k in range(chs - 1):
                        v = v + self.r3[k]
                    self.own[ch] = (v * scale).astype(self.own.dtype)
            elif stage == 5:
                most = self.own.at[pl.ds(0, chs - 1)]
                whole = pltpu.make_async_remote_copy(
                    src_ref=most, dst_ref=most, send_sem=send_sem.at[slot(self.i, 4)],
                    recv_sem=recv_sem.at[slot(self.i, 4)], device_id=(sp, ch), device_id_type=MESH)
                whole.wait_recv()
                sent.append(whole)
            elif stage == 6:
                self.copies[6][0].wait_recv()
                sent.append(self.copies[6][0])
            else:
                others = 2 * chips - 1 if self.r1 is None else chips - 1
                most = wg_out.at[pl.ds(self.base, others * self.u)]
                whole = pltpu.make_async_remote_copy(
                    src_ref=most, dst_ref=most, send_sem=send_sem.at[slot(self.i, 3)],
                    recv_sem=recv_sem.at[slot(self.i, 3)], device_id=(sp, ch), device_id_type=MESH)
                whole.wait_recv()
                sent.append(whole)
                self.local.wait()

    red_a = Reduce(0, r1a, None, r3a, own_a, mid_a)
    early = [Early(0, r1a, r2a), Early(1, r1d, r2d)]
    red_b = Reduce(1, None, r2b, r3b, own_b)
    red_c = Reduce(2, None, r2c, r3c, own_c)

    for lo, count, room in (
        (parts[0], 9 * ups, sub * 2 * chips),
        (parts[1], 9 * ups, sub * 2 * chips),
        (groups[1][0], 5 * ups, groups[1][1] * 2 * chips),
        (groups[2][0], 5 * ups, groups[2][1] * 2 * chips),
    ):
        if count < room:
            grad[lo + count:lo + room] = jnp.zeros((room - count, UNIT, LANES), jnp.float32)
    if 2 * sub < groups[0][1]:
        rest = mid_a.reshape(groups[0][1], UNIT, c_out)
        rest[2 * sub:] = jnp.zeros((groups[0][1] - 2 * sub, UNIT, LANES), jnp.float32)

    def all_sent():
        @pl.when(flat > 0)
        def _():
            halos[0].wait_send()
            halos[1].wait_send()

        for c in sent:
            c.wait_send()

    def halo_done(h):
        @pl.when(flat < last)
        def _():
            halos[h].wait_recv()

        @pl.when(flat == last)
        def _():
            h_nat[:, h * hc:(h + 1) * hc] = jnp.zeros((rows, hc, LANES), jnp.bfloat16)

    half = rows // 2
    both = [(2, mh), (0, mn)]

    wgrad(1, 0, mh)
    early[0].start(1)
    wgrad(2, 1, mh)
    early[1].start(1)
    early[0].finish(1)
    early[0].start(2)
    loads[2].wait()
    weights()
    early[1].finish(1)
    early[1].start(2)
    relay(0)
    dgrad(0, [(1, mh)], 0, 3)
    relay(1)
    dgrad(0, [(1, mh)], 3, half)
    early[0].finish(2)
    halo_done(0)
    spread_half(0)
    wgrad_half(0)
    red_b.start(2)

    early[1].finish(2)
    red_a.start(3)
    halo_done(1)
    spread_half(1)
    wgrad_half(1)
    red_c.start(2)
    red_a.finish(3)
    red_a.start(5)
    red_b.finish(2)
    red_b.start(3)
    dgrad(1, both, 0, 4)
    red_c.finish(2)
    red_c.start(3)
    red_a.finish(5)
    red_a.start(4)
    dgrad(1, both, 4, half)
    red_b.finish(3)
    red_b.start(4)
    red_c.finish(3)
    red_c.start(4)
    red_a.finish(4)
    red_a.start(6)
    red_a.finish(6)
    red_b.finish(4)
    red_c.finish(4)
    relay_done()
    all_sent()
    pltpu.make_async_copy(dg_v, dg_v, out_sem.at[0]).wait()


def store_kernel(groups, sub, ups, dg_in, wg_in, dg_out, wg_out, half_v, wide_v, sem):
    dg_copy = pltpu.make_async_copy(dg_in, dg_out, sem.at[0])
    dg_copy.start()
    load = pltpu.make_async_copy(wg_in, half_v, sem.at[1])
    load.start()
    load.wait()
    outs = []

    def send(tap0, taps, slot):
        here = pl.ds(tap0 * ups, taps * ups)
        outs.append(pltpu.make_async_copy(wide_v.at[here], wg_out.at[here], sem.at[slot]))
        outs[-1].start()

    for i in range(2):
        for j in range(-(-9 * ups // sub)):
            n = min(sub, 9 * ups - j * sub)
            src = groups[0][0] + j * groups[0][1] + i * sub
            wide_v[pl.ds(9 * (i + 1) * ups + j * sub, n)] = half_v[pl.ds(src, n)].astype(jnp.float32)
    send(9, 18, 2)
    lanes = half_v.shape[2]
    left = lax.broadcasted_iota(jnp.int32, (ups * UNIT, lanes), 1) < lanes // 2

    def block(h, q):
        v = half_v[pl.ds(groups[1 + h][0] + q * ups, ups)].astype(jnp.float32)
        return v.reshape(ups * UNIT, lanes)

    def put(tap, low, high):
        wide_v[pl.ds(tap * ups, ups)] = jnp.where(left, low, high).reshape(ups, UNIT, lanes)

    def other(v):
        return pltpu.roll(v, lanes // 2, 1)

    for q, kh in enumerate((1, 2, 0)):
        put(kh * 3 + 2, block(0, q), other(block(1, q)))
        put(kh * 3, other(block(0, q)), block(1, q))
    put(4, block(0, 3), other(block(1, 3)))
    put(7, other(block(0, 3)), block(1, 3))
    put(1, block(0, 4), other(block(1, 4)))
    send(0, 9, 3)
    dg_copy.wait()
    for c in outs:
        c.wait()


def on_device(features, pre_act, cotangent, weight):
    c_in, planes_in, _, _, rows, cols = features.shape
    c_out, planes = pre_act.shape[:2]
    taps = weight.shape[0]
    chips = lax.axis_size("sp") // 2
    chs = lax.axis_size("ch")
    devices = chips * 2 * chs
    scale = 1.0 / math.sqrt(devices * planes * rows * cols)
    ups = c_in // UNIT
    sub = -(-9 * ups // (2 * chips))
    u_a = -(-2 * sub // chs) * chs
    u_b = -(-5 * ups // (2 * chips))
    span_b = u_b * 2 * chips
    groups = ((2 * span_b, u_a), (0, u_b), (span_b, u_b))
    units = u_a * 2 * chips + 2 * span_b
    parts = (2 * span_b, 2 * span_b + sub * 2 * chips)
    cfg = (chips, chs, rows, c_in, c_out, scale, groups, parts, sub)
    bf, f32 = jnp.bfloat16, jnp.float32
    span = rows * cols
    any_spec = pl.BlockSpec(memory_space=pl.ANY)

    def part(*lead, dtype=f32):
        return pltpu.VMEM(lead + (UNIT, c_out), dtype)

    held = 2 * units + (u_a + 2 * u_b) * (2 * chips + chs)
    vmem = 18 * 2**20 + held * UNIT * c_out * 4
    dg, wg = pl.pallas_call(
        functools.partial(kernel, cfg),
        out_shape=(
            jax.ShapeDtypeStruct((c_in, 2, 2, rows, 2, cols), bf),
            jax.ShapeDtypeStruct((units, UNIT, c_out), bf),
        ),
        in_specs=[pl.BlockSpec(memory_space=pltpu.HBM)] * 4,
        out_specs=(any_spec, any_spec),
        scratch_shapes=[
            pltpu.VMEM((rows, c_out, cols), bf),
            pltpu.VMEM((rows, c_out, cols), bf),
            pltpu.VMEM((2, 2, rows, c_in, 2, cols), bf),
            pltpu.VMEM(weight.shape, bf),
            pltpu.VMEM((rows, c_out, cols), bf),
            pltpu.VMEM((rows, c_out, cols), bf),
            pltpu.VMEM((2 * c_out, span + cols), bf),
            pltpu.VMEM((2 * c_out, span + cols), bf),
            pltpu.VMEM((2, 4 * c_in, span), bf),
            pltpu.VMEM((3, 6 * c_in, 2 * c_out), bf),
            pltpu.VMEM((2, 2 * c_in, c_out), f32),
            pltpu.VMEM((2, 6 * c_in, c_out), f32),
            pltpu.VMEM((2, 2, rows, c_in, 2, cols), bf),
            part(units),
            part(chs, u_a // chs, dtype=bf),
            part(u_b, dtype=bf),
            part(u_b, dtype=bf),
            part(sub * chips),
            part(sub * chips),
            part(chips - 1, sub),
            part(chips - 1, sub),
            part(2 * chips - 1, u_b),
            part(2 * chips - 1, u_b),
            part(chs, u_a // chs),
            part(chs - 1, u_a // chs),
            part(chs, u_b),
            part(chs, u_b),
            pltpu.VMEM((2 * rows, c_out // 2, cols), bf),
            pltpu.SemaphoreType.DMA((4,)),
            pltpu.SemaphoreType.DMA((4,)),
            pltpu.SemaphoreType.DMA((2,)),
            pltpu.SemaphoreType.DMA((2,)),
            pltpu.SemaphoreType.DMA((2,)),
            pltpu.SemaphoreType.DMA((2,)),
            pltpu.SemaphoreType.DMA((14,)),
            pltpu.SemaphoreType.DMA((14,)),
        ],
        compiler_params=pltpu.CompilerParams(
            collective_id=0, has_side_effects=True, vmem_limit_bytes=vmem
        ),
    )(
        pltpu.with_memory_space_constraint(pre_act.transpose(1, 2, 0, 3), pltpu.HBM),
        pltpu.with_memory_space_constraint(cotangent.transpose(1, 2, 0, 3), pltpu.HBM),
        pltpu.with_memory_space_constraint(features.transpose(0, 1, 2, 4, 3, 5), pltpu.HBM),
        pltpu.with_memory_space_constraint(weight, pltpu.HBM),
    )
    dg, wg = pl.pallas_call(
        functools.partial(store_kernel, groups, sub, ups),
        out_shape=(
            jax.ShapeDtypeStruct((c_in, planes_in, 2, rows, 2, cols), bf),
            jax.ShapeDtypeStruct((taps * ups, UNIT, c_out), f32),
        ),
        in_specs=[any_spec] * 2,
        out_specs=(pl.BlockSpec(memory_space=pltpu.HBM),) * 2,
        scratch_shapes=[
            part(units, dtype=bf),
            part(taps * ups),
            pltpu.SemaphoreType.DMA((4,)),
        ],
        compiler_params=pltpu.CompilerParams(vmem_limit_bytes=2**20 + (units + 2 * taps * ups) * UNIT * c_out * 2),
    )(dg, wg)
    return dg.transpose(0, 1, 2, 4, 3, 5), wg.reshape(taps, c_in, c_out)


def solution(mesh):
    return jax.shard_map(
        on_device,
        mesh=mesh,
        in_specs=(
            P(None, ("sp", "ch"), None, None, None, None),
            P(None, ("sp", "ch"), None, None),
            P(None, ("sp", "ch"), None, None),
            P(),
        ),
        out_specs=(P(None, ("sp", "ch"), None, None, None, None), P()),
        check_vma=False,
    )
```
